32 devices in a mesh: band: 4 (over z), dom: 8 (over y, x, core).
Axes of the slice: x: 2, y: 2, z: 4, core: 2. Of those that a mesh axis runs over, the one named last changes fastest.
Arguments:
- response: float32 [4, 256, 32, 8, 128], P(None, 'band', 'dom'), may hold values from -6 to 6
- occupied: float32 [256, 32, 8, 128], P('band', 'dom'), may hold values from -6 to 6
- locked_set: bfloat16 [4096, 32, 8, 128], P(None, 'dom'), may hold values from -0.03125 to 0.03125
- potential: float32 [32, 8, 128], P('dom'), may hold values from -1.5 to 0
- perturbation: float32 [4, 32, 8, 128], P(None, 'dom'), may hold values from -30 to 30
- xc_kernel: float32 [32, 8, 128], P('dom'), may hold values from 0.005 to 0.03
- energies: float32 [256], P('band'), may hold values from -1 to -0.2
- first_step: float32 [4, 256], P(None, 'band'), may hold values from 0.03 to 0.1
- second_step: float32 [4, 256], P(None, 'band'), may hold values from 0.03 to 0.1
Outputs:
- new_response: float32 [4, 256, 32, 8, 128], P(None, 'band', 'dom')
- response_potential: float32 [4, 32, 8, 128], P(None, 'dom')
The draws below stay inside these ranges and needn't reach their ends.
All inputs are finite; a program needn't handle non-finite values.
Results may differ from the reference program's by a relative error of at most 0.007.
Values may be sent and summed in bfloat16 or wider, within the bound.
No kernel may reach another device: no remote copies, remote signals or barrier semaphores. Data moves between devices by JAX's collectives and lax.ppermute only.
A program may use at most 256 MiB of HBM per device.

```python
import math
import jax
import jax.numpy as jnp
from jax import lax

GZ = 8
GY = 128
PERT = 4
ORBS = 256
LOCKED = 4096
GX = 32
N_DOM = 8


def draw_perturbation(key, part):
    grid_shape = (PERT, GX, GZ, GY)
    position = jnp.arange(GX, dtype=jnp.float32)[None, :, None, None] / max(GX - 1, 1)
    envelope = 1.5 * jnp.exp(jnp.log(5.0) * position)
    fluctuation = jnp.clip(jax.random.normal(key, grid_shape, jnp.float32), -4.0, 4.0)
    return (fluctuation * envelope).astype(jnp.float32)


def level_of(own_key, extent, shards, smallest, largest):
    def one(dim, blocks):
        steps = jax.random.uniform(jax.random.fold_in(jax.random.fold_in(own_key, 6), dim), (blocks,), jnp.float32, smallest / len(shards), largest / len(shards))
        return jnp.repeat(jnp.exp(steps), extent[dim] // blocks).reshape((-1,) + (1,) * (len(extent) - dim - 1))

    loudness = one(*shards[0])
    for cut in shards[1:]:
        loudness = loudness * one(*cut)
    return loudness


def normal_values(own_key, extent, scale, limit, shards=(), held_as=jnp.bfloat16):
    values = scale * jax.random.normal(own_key, extent, jnp.float32)
    if shards:
        values = values * level_of(own_key, extent, shards, -0.22, 0.18)
    return jnp.clip(values, -limit, limit).astype(held_as)


def setup_inputs(seed: int = 0) -> dict:
    streams_of = jax.random.split(jax.random.key(seed), 10)
    response = normal_values(streams_of[0], (PERT, ORBS, GX, GZ, GY), 1.0, 6.0, ((1, 4), (2, 8)), jnp.float32)
    occupied = normal_values(streams_of[1], (ORBS, GX, GZ, GY), 1.0, 6.0, ((0, 4), (1, 8)), jnp.float32)
    locked_set = normal_values(streams_of[2], (LOCKED, GX, GZ, GY), (GX * GZ * GY) ** -0.5, 0.03125, ((1, 8),))
    potential = jnp.clip(-1.5 + 1.5 * jax.random.uniform(streams_of[3], (GX, GZ, GY), jnp.float32) ** level_of(streams_of[3], (GX, GZ, GY), ((0, 8),), -0.2, 0.2), -1.5, 0.0)
    perturbation = draw_perturbation(jax.random.fold_in(streams_of[9], 71), 0)
    xc_kernel = jnp.clip(jnp.exp(math.log(0.03) - 1.7917595 * jax.random.uniform(streams_of[5], (GX, GZ, GY), jnp.float32) ** level_of(streams_of[5], (GX, GZ, GY), ((0, 8),), -0.2, 0.2)), 0.005, 0.03)
    energies = jnp.clip(-1.0 + 0.8 * jax.random.uniform(streams_of[6], (ORBS,), jnp.float32) ** level_of(streams_of[6], (ORBS,), ((0, 4),), -0.2, 0.2), -1.0, -0.2)
    first_step = jnp.clip(jnp.exp(math.log(0.1) - 1.2039728 * jax.random.uniform(streams_of[7], (PERT, ORBS), jnp.float32) ** level_of(streams_of[7], (PERT, ORBS), ((1, 4),), -0.2, 0.2)), 0.03, 0.1)
    second_step = jnp.clip(jnp.exp(math.log(0.1) - 1.2039728 * jax.random.uniform(streams_of[8], (PERT, ORBS), jnp.float32) ** level_of(streams_of[8], (PERT, ORBS), ((1, 4),), -0.2, 0.2)), 0.03, 0.1)
    return {"response": response, "occupied": occupied, "locked_set": locked_set, "potential": potential, "perturbation": perturbation, "xc_kernel": xc_kernel, "energies": energies, "first_step": first_step, "second_step": second_step}


near_weight = 4.0 / 3.0
far_weight = -1.0 / 12.0
centre_weight = -7.5


def laplace(grid_field):
    result = centre_weight * grid_field
    for axis_pos in (-3, -1):
        result = result + near_weight * (jnp.roll(grid_field, 1, axis_pos) + jnp.roll(grid_field, -1, axis_pos))
        result = result + far_weight * (jnp.roll(grid_field, 2, axis_pos) + jnp.roll(grid_field, -2, axis_pos))
    widths = [(0, 0)] * (grid_field.ndim - 2) + [(2, 2), (0, 0)]
    zpadded = jnp.pad(grid_field, widths)
    result = result + near_weight * (zpadded[..., 3:-1, :] + zpadded[..., 1:-3, :])
    result = result + far_weight * (zpadded[..., 4:, :] + zpadded[..., :-4, :])
    return result


def hamiltonian(grid_field, potential, energies):
    return -0.5 * laplace(grid_field) + potential * grid_field - energies[None, :, None, None, None] * grid_field


def project(rhs_field, locked_set):
    columns = rhs_field.shape[0] * rhs_field.shape[1]
    flattened = rhs_field.reshape(columns, -1)
    rounded = flattened.astype(jnp.bfloat16)
    locked_flat = locked_set.reshape(locked_set.shape[0], -1)
    slab_rounded = jnp.moveaxis(rounded.reshape(columns, N_DOM, -1), 1, 0)
    slab_locked = jnp.moveaxis(locked_flat.reshape(locked_flat.shape[0], N_DOM, -1), 1, 0)

    def add_slab(total, pieces):
        locked_piece, rounded_piece = pieces
        partial_value = jnp.dot(locked_piece, rounded_piece.T, preferred_element_type=jnp.float32)
        partial_b = lax.optimization_barrier(partial_value.astype(jnp.bfloat16))
        return total + partial_b.astype(jnp.float32), None

    start = jnp.zeros((locked_flat.shape[0], columns), jnp.float32)
    margin, _ = lax.scan(add_slab, start, (slab_locked, slab_rounded))
    margin_b = margin.astype(jnp.bfloat16)
    removed = jnp.dot(margin_b.T, locked_flat, preferred_element_type=jnp.float32)
    return (flattened - removed).reshape(rhs_field.shape)


def reference(response, occupied, locked_set, potential, perturbation, xc_kernel, energies, first_step, second_step):
    first_rhs = -(perturbation[:, None] * occupied[None]) - hamiltonian(response, potential, energies)
    first_res = project(first_rhs, locked_set)
    middle = response + first_step[:, :, None, None, None] * first_res
    first_norm = jnp.sum(first_res * first_res, axis=(2, 3, 4))
    density = 2.0 * jnp.sum(occupied[None] * middle, axis=1)
    response_potential = perturbation - xc_kernel[None] * density
    second_rhs = -(response_potential[:, None] * occupied[None]) - hamiltonian(middle, potential, energies)
    second_res = project(second_rhs, locked_set)
    second_norm = jnp.sum(second_res * second_res, axis=(2, 3, 4))
    fletcher_ratio = second_norm / first_norm
    direction = second_res + fletcher_ratio[:, :, None, None, None] * first_res
    new_response = middle + second_step[:, :, None, None, None] * direction
    return new_response, response_potential
```

```python
import jax
import jax.numpy as jnp
from jax import lax
from jax.experimental import pallas as pl
from jax.experimental.pallas import tpu as pltpu
from jax.sharding import PartitionSpec as P

f32 = jnp.float32
bf16 = jnp.bfloat16
near_half = 2.0 / 3.0
far_half = -1.0 / 24.0
centre_half = -3.75
halo_parts = 1
MIB = 1 << 20


def onchip(array):
    return pltpu.with_memory_space_constraint(array, pltpu.VMEM)


def run(body, args, outs, scratch=(), aliases=None, limit=8, name=None):
    kinds = {"v": pltpu.VMEM, "s": pltpu.SMEM, "a": pl.ANY}
    results = pl.pallas_call(
        body,
        in_specs=[pl.BlockSpec(memory_space=kinds[kind]) for _, kind in args],
        out_specs=[pl.BlockSpec(memory_space=pltpu.VMEM) for _ in outs],
        out_shape=[
            pltpu.VMEM(shape, dtype) if kept and name == "relay" else jax.ShapeDtypeStruct(shape, dtype)
            for shape, dtype, kept in outs
        ],
        scratch_shapes=list(scratch),
        input_output_aliases=aliases or {},
        compiler_params=pltpu.CompilerParams(vmem_limit_bytes=limit * MIB),
        name=name,
    )(*[array for array, _ in args])
    return [onchip(r) if kept and name == "relay" else r for r, (_, _, kept) in zip(results, outs)]


def tree_sum(terms):
    while len(terms) > 1:
        terms = [terms[i] + terms[i + 1] for i in range(0, len(terms), 2)]
    return terms[0]


def per_row(scalars, row, width):
    line = scalars[row : row + 1, :]
    return jnp.broadcast_to(line, (width, line.shape[1])).T


def dot_nt(a, b):
    return lax.dot_general(a, b, (((1,), (1,)), ((), ())), preferred_element_type=f32)


def dot_nn(a, b):
    return lax.dot_general(a, b, (((1,), (0,)), ((), ())), preferred_element_type=f32)


def local(
    response,
    occupied,
    locked_set,
    potential,
    perturbation,
    xc_kernel,
    energies,
    first_step,
    second_step,
):
    perts, orbs, planes, gz, gy = response.shape
    locked = locked_set.shape[0]
    columns = perts * orbs
    cells = planes * gz * gy
    stripe = planes * gy
    doms = lax.axis_size("dom")
    bands = lax.axis_size("band")
    chips = doms // 2
    half = locked // 2
    piece = half // chips
    part_z = gz // halo_parts
    part_cells = part_z * stripe
    part_edge = part_z * 2 * gy
    position = lax.axis_index("dom")
    where = jnp.stack([position & 1, position >> 1])

    def col(z, x):
        return (z * planes + x) * gy

    def edge(z, k):
        return (z * 2 + k) * gy

    def swap(array, mask, axis):
        count = lax.axis_size(axis)
        return lax.ppermute(array, axis, [(i, i ^ mask) for i in range(count)])

    ahead = [(i, (i + 1) % doms) for i in range(doms)]
    behind = [((i + 1) % doms, i) for i in range(doms)]

    scalars = jnp.stack(
        [jnp.tile(energies, perts), first_step.reshape(columns), second_step.reshape(columns)]
    )

    def flatten_body(source, early, placed, flat, *edges):
        def rows_step(p, carry):
            rows = pl.ds(pl.multiple_of(p * orbs, orbs), orbs)
            for x in range(planes):
                wide = source[rows, x].reshape(orbs, gz * gy)
                for z in range(gz):
                    value = wide[:, z * gy : (z + 1) * gy]
                    flat[rows, col(z, x) : col(z, x) + gy] = value
                    part, inner = divmod(z, part_z)
                    if x < 2:
                        at = edge(inner, x)
                        edges[2 * part][rows, at : at + gy] = value.astype(bf16)
                    if x >= planes - 2:
                        at = edge(inner, x - planes + 2)
                        edges[2 * part + 1][rows, at : at + gy] = value.astype(bf16)
            return carry

        lax.fori_loop(0, source.shape[0] // orbs, rows_step, 0)

    flat_response, *edges1 = run(
        flatten_body,
        [(response.reshape(columns, planes, gz, gy), "v"), (scalars, "a"), (where, "a")],
        [((columns, cells), f32, True)]
        + [((columns, part_edge), bf16, False)] * (2 * halo_parts),
        limit=8,
        name="flatten",
    )

    def halos_of(edges):
        received = []
        for part in range(halo_parts):
            low = lax.ppermute(edges[2 * part + 1], "dom", ahead)
            high = lax.ppermute(edges[2 * part], "dom", behind)
            received.append((low, high))
        return received

    halos1 = halos_of(edges1)


    def setup_body(occ, pot, pert, xc, occ_flat, pot_flat, pert_flat, xc_flat):
        for x in range(planes):
            wide = occ[:, x].reshape(orbs, gz * gy)
            for z in range(gz):
                cut = slice(col(z, x), col(z, x) + gy)
                occ_flat[:, cut] = wide[:, z * gy : (z + 1) * gy]
                pot_flat[0:1, cut] = pot[x, z : z + 1, :]
                xc_flat[0:1, cut] = xc[x, z : z + 1, :]
                for p in range(perts):
                    pert_flat[p, 0:1, cut] = pert[p, x, z : z + 1, :]

    flat_occupied, flat_potential, flat_perturbation, flat_xc = run(
        setup_body,
        [(occupied, "v"), (potential, "v"), (perturbation, "v"), (xc_kernel, "v")],
        [
            ((orbs, cells), f32, True),
            ((1, cells), f32, True),
            ((perts, 1, cells), f32, True),
            ((1, cells), f32, True),
        ],
        limit=2,
        name="setup",
    )

    chunk = min(256, locked)
    chunks = locked // chunk

    def relay_body(source, target, held, sems):
        def copy(i):
            slot = lax.rem(i, 3)
            rows = pl.ds(pl.multiple_of(i * chunk, chunk), chunk)
            return pltpu.make_async_copy(source.at[rows], held.at[slot], sems.at[slot])

        copy(0).start()
        copy(1).start()

        def step(i, carry):
            @pl.when(i + 2 < chunks)
            def _():
                copy(i + 2).start()

            copy(i).wait()
            slot = lax.rem(i, 3)
            rows = pl.ds(pl.multiple_of(i * chunk, chunk), chunk)
            for x in range(planes):
                wide = held[slot, :, x].reshape(chunk, gz * gy)
                for z in range(gz):
                    target[rows, col(z, x) : col(z, x) + gy] = wide[:, z * gy : (z + 1) * gy]
            return carry

        lax.fori_loop(0, chunks, step, 0)

    (locked_flat,) = run(
        relay_body,
        [(locked_set, "a")],
        [((locked, cells), bf16, True)],
        scratch=[
            pltpu.VMEM((3, chunk, planes, gz, gy), bf16),
            pltpu.SemaphoreType.DMA((3,)),
        ],
        limit=7,
        name="relay",
    )

    def stencil_body(field, pot, scal, out, energy):
        energy[...] = per_row(scal, 0, gy)
        block = 32

        def rows_step(i, carry):
            rows = pl.ds(pl.multiple_of(i * block, block), block)
            base = energy[rows, :] + centre_half

            def at(z, x):
                return field[rows, col(z, x) : col(z, x) + gy]

            for z in range(gz):
                for x in range(planes):
                    here = at(z, x)
                    near = pltpu.roll(here, 1, 1) + pltpu.roll(here, gy - 1, 1)
                    far = pltpu.roll(here, 2, 1) + pltpu.roll(here, gy - 2, 1)
                    for d in (-1, 1):
                        if 0 <= x + d < planes:
                            near = near + at(z, x + d)
                        if 0 <= z + d < gz:
                            near = near + at(z + d, x)
                        if 0 <= x + 2 * d < planes:
                            far = far + at(z, x + 2 * d)
                        if 0 <= z + 2 * d < gz:
                            far = far + at(z + 2 * d, x)
                    own = base - pot[0:1, col(z, x) : col(z, x) + gy]
                    out[rows, col(z, x) : col(z, x) + gy] = (
                        own * here + near_half * near + far_half * far
                    )
            return carry

        lax.fori_loop(0, columns // block, rows_step, 0)

    def stencil(field):
        (out,) = run(
            stencil_body,
            [(field, "v"), (flat_potential, "v"), (scalars, "v")],
            [((columns, cells), f32, True)],
            scratch=[pltpu.VMEM((columns, gy), f32)],
            limit=1,
            name="stencil",
        )
        return out

    def finish_rhs(part, partial, low, high, occ, pot, rhs, rounded):
        first = part * part_z

        def rows_step(p, carry):
            rows = pl.ds(pl.multiple_of(p * orbs, orbs), orbs)
            for inner in range(part_z):
                for x in range(planes):
                    at = col(first + inner, x)
                    value = partial[rows, at : at + gy] - pot[p, 0:1, at : at + gy] * occ[
                        :, at : at + gy
                    ]

                    def halo(ref, k):
                        start = edge(inner, k)
                        return ref[rows, start : start + gy].astype(f32)

                    if x == 0:
                        value = value + (near_half * halo(low, 1) + far_half * halo(low, 0))
                    if x == 1:
                        value = value + far_half * halo(low, 1)
                    if x == planes - 2:
                        value = value + far_half * halo(high, 0)
                    if x == planes - 1:
                        value = value + (near_half * halo(high, 0) + far_half * halo(high, 1))
                    rhs[rows, at : at + gy] = value
                    rounded[rows, at : at + gy] = value.astype(bf16)
            return carry

        lax.fori_loop(0, perts, rows_step, 0)

    def margins(partial, halos, pot):
        low, high = halos[0]

        def other_body(where_ref, part_ref, low_ref, high_ref, occ, pot_ref, lock, rhs, rounded, out):
            finish_rhs(0, part_ref, low_ref, high_ref, occ, pot_ref, rhs, rounded)
            start = (1 - where_ref[0]) * half
            for m in range(chips):
                rows = pl.ds(pl.multiple_of(start + (where_ref[1] ^ m) * piece, piece), piece)
                out[:, m * piece : (m + 1) * piece] = dot_nt(rounded[...], lock[rows, :]).astype(bf16)

        rhs, rounded, other = run(
            other_body,
            [
                (where, "s"),
                (partial, "v"),
                (low, "v"),
                (high, "v"),
                (flat_occupied, "v"),
                (pot, "v"),
                (locked_flat, "v"),
            ],
            [
                ((columns, cells), f32, True),
                ((columns, cells), bf16, True),
                ((columns, half), bf16, False),
            ],
            aliases={1: 0},
            limit=2,
            name="margin_other",
        )
        arrived = swap(other, 1, "dom")

        def own_body(where_ref, rounded_ref, lock, arrived_ref, kept, *sent):
            start = where_ref[0] * half
            for m in reversed(range(chips)):
                rows = pl.ds(pl.multiple_of(start + (where_ref[1] ^ m) * piece, piece), piece)
                value = dot_nt(rounded_ref[...], lock[rows, :])
                value = value + arrived_ref[:, m * piece : (m + 1) * piece].astype(f32)
                if m == 0:
                    kept[...] = value
                else:
                    sent[m - 1][...] = value.astype(bf16)

        kept, *sent = run(
            own_body,
            [(where, "s"), (rounded, "v"), (locked_flat, "v"), (arrived, "v")],
            [((columns, piece), f32, False)]
            + [((columns, piece), bf16, False)] * (chips - 1),
            limit=2,
            name="margin_own",
        )
        arrivals = [swap(sent[m - 1], 2 * m, "dom") for m in range(1, chips)]

        def add_body(*refs):
            out = refs[-1]
            out[...] = tree_sum([r[...].astype(f32) for r in refs[:-1]]).astype(bf16)

        (mine,) = run(
            add_body,
            [(kept, "v")] + [(r, "v") for r in arrivals],
            [((columns, piece), bf16, False)],
            limit=2,
            name="add_pieces",
        )
        gathered = [mine] + [swap(mine, 2 * m, "dom") for m in range(1, chips)]
        return rhs, gathered

    def collect(where_ref, pieces, held):
        for m, ref in enumerate(pieces):
            at = pl.ds(pl.multiple_of((where_ref[1] ^ m) * piece, piece), piece)
            held[:, at] = ref[...]

    def remove_own(gathered):
        def body(where_ref, *refs):
            pieces, (lock, acc, held) = refs[:chips], refs[chips:]
            collect(where_ref, pieces, held)
            rows = pl.ds(pl.multiple_of(where_ref[0] * half, half), half)

            def step(z, carry):
                at = pl.ds(pl.multiple_of(z * stripe, stripe), stripe)
                acc[:, at] = dot_nn(held[...], lock[rows, at])
                return carry

            lax.fori_loop(0, gz, step, 0)

        (acc,) = run(
            body,
            [(where, "s")] + [(g, "v") for g in gathered] + [(locked_flat, "v")],
            [((columns, cells), f32, True)],
            scratch=[pltpu.VMEM((columns, half), bf16)],
            limit=2,
            name="remove_own",
        )
        return acc

    def line_of(lanes):
        return jnp.sum(lanes.T, axis=0, keepdims=True)

    def squares(value):
        total = value[:, :gy] * value[:, :gy]
        for x in range(1, planes):
            total = total + value[:, x * gy : (x + 1) * gy] * value[:, x * gy : (x + 1) * gy]
        return total

    def first_finish(others, acc, rhs, field):
        def body(where_ref, *refs):
            pieces = refs[:chips]
            lock, acc_ref, rhs_ref, field_ref, occ, scal = refs[chips : chips + 6]
            res, mid, low, high, dens, norm = refs[chips + 6 : chips + 12]
            held, step_rows, lanes = refs[chips + 12 :]
            collect(where_ref, pieces, held)
            step_rows[...] = per_row(scal, 1, gy)
            lanes[...] = jnp.zeros_like(lanes)
            rows = pl.ds(pl.multiple_of((1 - where_ref[0]) * half, half), half)

            def step(z, carry):
                at = pl.ds(pl.multiple_of(z * stripe, stripe), stripe)
                removed = acc_ref[:, at] + dot_nn(held[...], lock[rows, at])
                value = rhs_ref[:, at] - removed
                res[:, at] = value
                lanes[...] += squares(value)
                for x in range(planes):
                    cut = slice(x * gy, (x + 1) * gy)
                    spot = pl.ds(pl.multiple_of(z * stripe + x * gy, gy), gy)
                    new = field_ref[:, spot] + step_rows[...] * value[:, cut]
                    mid[:, spot] = new
                    weight = 2.0 * occ[:, spot]
                    sums = [
                        jnp.sum(weight * new[p * orbs : (p + 1) * orbs], axis=0, keepdims=True)
                        for p in range(perts)
                    ]
                    dens[:, spot] = jnp.concatenate(sums, axis=0).astype(bf16)
                    if x < 2:
                        place = pl.ds(pl.multiple_of((z * 2 + x) * gy, gy), gy)
                        low[:, place] = new.astype(bf16)
                    if x >= planes - 2:
                        place = pl.ds(pl.multiple_of((z * 2 + x - planes + 2) * gy, gy), gy)
                        high[:, place] = new.astype(bf16)
                return carry

            lax.fori_loop(0, gz, step, 0)
            norm[...] = line_of(lanes[...])

        return run(
            body,
            [(where, "s")]
            + [(g, "v") for g in others]
            + [
                (locked_flat, "v"),
                (acc, "v"),
                (rhs, "v"),
                (field, "v"),
                (flat_occupied, "v"),
                (scalars, "v"),
            ],
            [
                ((columns, cells), f32, True),
                ((columns, cells), f32, True),
                ((columns, gz * 2 * gy), bf16, False),
                ((columns, gz * 2 * gy), bf16, False),
                ((perts, cells), bf16, False),
                ((1, columns), f32, False),
            ],
            scratch=[
                pltpu.VMEM((columns, half), bf16),
                pltpu.VMEM((columns, gy), f32),
                pltpu.VMEM((columns, gy), f32),
            ],
            aliases={chips + 3: 0, chips + 4: 1},
            limit=5,
            name="first_finish",
        )

    def second_finish(others, acc, rhs):
        def body(where_ref, *refs):
            pieces = refs[:chips]
            lock, acc_ref, rhs_ref, res, norm, held, lanes = refs[chips:]
            collect(where_ref, pieces, held)
            lanes[...] = jnp.zeros_like(lanes)
            rows = pl.ds(pl.multiple_of((1 - where_ref[0]) * half, half), half)

            def step(z, carry):
                at = pl.ds(pl.multiple_of(z * stripe, stripe), stripe)
                removed = acc_ref[:, at] + dot_nn(held[...], lock[rows, at])
                value = rhs_ref[:, at] - removed
                res[:, at] = value
                lanes[...] += squares(value)
                return carry

            lax.fori_loop(0, gz, step, 0)
            norm[...] = line_of(lanes[...])

        return run(
            body,
            [(where, "s")]
            + [(g, "v") for g in others]
            + [(locked_flat, "v"), (acc, "v"), (rhs, "v")],
            [((columns, cells), f32, True), ((1, columns), f32, False)],
            scratch=[pltpu.VMEM((columns, half), bf16), pltpu.VMEM((columns, gy), f32)],
            aliases={chips + 3: 0},
            limit=2,
            name="second_finish",
        )

    def across(array, axis):
        return [array] + [swap(array, m, axis) for m in range(1, lax.axis_size(axis))]

    def norm_terms(norm):
        other = swap(norm, 1, "dom")

        def body(one, two, out):
            out[...] = one[...] + two[...]

        (pair,) = run(
            body, [(norm, "v"), (other, "v")], [((1, columns), f32, False)], limit=1, name="pair"
        )
        return [pair] + [swap(pair, 2 * m, "dom") for m in range(1, chips)]

    partial1 = stencil(flat_response)
    rhs1, gathered1 = margins(partial1, halos1, flat_perturbation)
    others1 = [swap(g, 1, "dom") for g in gathered1]
    acc1 = remove_own(gathered1)
    first_res, middle, low_edge, high_edge, dens, norm1 = first_finish(
        others1, acc1, rhs1, flat_response
    )
    halos2 = halos_of([low_edge, high_edge])
    densities = across(dens, "band")
    norms1 = norm_terms(norm1)

    def potential_body(*refs):
        parts, squares1 = refs[:bands], refs[bands : bands + chips]
        pert, xc, flat, native, norm = refs[bands + chips :]
        norm[...] = tree_sum([r[...] for r in squares1])
        density = tree_sum([r[...].astype(f32) for r in parts])
        for z in range(gz):
            for x in range(planes):
                cut = slice(col(z, x), col(z, x) + gy)
                for p in range(perts):
                    value = pert[p, 0:1, cut] - xc[0:1, cut] * density[p : p + 1, cut]
                    flat[p, 0:1, cut] = value
                    native[p, x, z : z + 1, :] = value

    flat_rp, response_potential, first_norm = run(
        potential_body,
        [(d, "v") for d in densities]
        + [(n, "v") for n in norms1]
        + [(flat_perturbation, "v"), (flat_xc, "v")],
        [
            ((perts, 1, cells), f32, True),
            ((perts, planes, gz, gy), f32, False),
            ((1, columns), f32, True),
        ],
        limit=1,
        name="potential",
    )

    partial2 = stencil(middle)
    rhs2, gathered2 = margins(partial2, halos2, flat_rp)
    others2 = [swap(g, 1, "dom") for g in gathered2]
    acc2 = remove_own(gathered2)
    second_res, norm2 = second_finish(others2, acc2, rhs2)
    norms2 = norm_terms(norm2)

    def final_body(*refs):
        twos = refs[:chips]
        one, mid, res1, res2, scal, out, steps, blends = refs[chips:]
        ratio = tree_sum([r[...] for r in twos]) / one[...]
        blend = scal[2:3, :] * ratio
        steps[...] = per_row(scal, 2, gy)
        blends[...] = jnp.broadcast_to(blend, (gy, columns)).T
        block = 64 if columns % 64 == 0 else columns

        def rows_step(i, carry):
            rows = pl.ds(pl.multiple_of(i * block, block), block)
            step, mix = steps[rows, :], blends[rows, :]
            for x in range(planes):
                values = []
                for z in range(gz):
                    cut = slice(col(z, x), col(z, x) + gy)
                    values.append(mid[rows, cut] + step * res2[rows, cut] + mix * res1[rows, cut])
                out[rows, x] = jnp.concatenate(values, axis=1).reshape(block, gz, gy)
            return carry

        lax.fori_loop(0, columns // block, rows_step, 0)

    (new_response,) = run(
        final_body,
        [(n, "v") for n in norms2]
        + [(first_norm, "v"), (middle, "v"), (first_res, "v"), (second_res, "v"), (scalars, "v")],
        [((columns, planes, gz, gy), f32, False)],
        scratch=[pltpu.VMEM((columns, gy), f32), pltpu.VMEM((columns, gy), f32)],
        limit=5,
        name="final",
    )
    return new_response.reshape(response.shape), response_potential


def solution(mesh):
    placed = (
        P(None, "band", "dom", None, None),
        P("band", "dom", None, None),
        P(None, "dom", None, None),
        P("dom", None, None),
        P(None, "dom", None, None),
        P("dom", None, None),
        P("band"),
        P(None, "band"),
        P(None, "band"),
    )
    return jax.shard_map(
        local,
        mesh=mesh,
        in_specs=placed,
        out_specs=(P(None, "band", "dom", None, None), P(None, "dom", None, None)),
        check_vma=False,
    )
```

```python
import jax
import jax.numpy as jnp
from jax import lax
from jax.experimental import pallas as pl
from jax.experimental.pallas import tpu as pltpu
from jax.sharding import PartitionSpec as P

f32 = jnp.float32
bf16 = jnp.bfloat16
near_half = 2.0 / 3.0
far_half = -1.0 / 24.0
centre_half = -3.75
halo_parts = 1
MIB = 1 << 20


def run(body, args, outs, scratch=(), aliases=None, limit=8, name=None):
    kinds = {"v": pltpu.VMEM, "s": pltpu.SMEM, "a": pl.ANY, "h": pltpu.HBM}
    results = pl.pallas_call(
        body,
        in_specs=[pl.BlockSpec(memory_space=kinds[kind]) for _, kind in args],
        out_specs=[pl.BlockSpec(memory_space=kinds[out[2] if len(out) > 2 else "v"]) for out in outs],
        out_shape=[jax.ShapeDtypeStruct(out[0], out[1]) for out in outs],
        scratch_shapes=list(scratch),
        input_output_aliases=aliases or {},
        compiler_params=pltpu.CompilerParams(vmem_limit_bytes=limit * MIB),
        name=name,
    )(*[array for array, _ in args])
    return list(results)


def tree_sum(terms):
    while len(terms) > 1:
        terms = [terms[i] + terms[i + 1] for i in range(0, len(terms), 2)]
    return terms[0]


def per_row(scalars, row, width):
    line = scalars[row : row + 1, :]
    return jnp.broadcast_to(line, (width, line.shape[1])).T


def dot_nt(a, b):
    return lax.dot_general(a, b, (((1,), (1,)), ((), ())), preferred_element_type=f32)


def dot_nn(a, b):
    return lax.dot_general(a, b, (((1,), (0,)), ((), ())), preferred_element_type=f32)


def local(
    response,
    occupied,
    locked_set,
    potential,
    perturbation,
    xc_kernel,
    energies,
    first_step,
    second_step,
):
    perts, orbs, planes, gz, gy = response.shape
    locked = locked_set.shape[0]
    columns = perts * orbs
    cells = planes * gz * gy
    stripe = planes * gy
    doms = lax.axis_size("dom")
    bands = lax.axis_size("band")
    chips = doms // 2
    half = locked // 2
    piece = half // chips
    part_z = gz // halo_parts
    part_cells = part_z * stripe
    part_edge = part_z * 2 * gy
    position = lax.axis_index("dom")
    where = jnp.stack([position & 1, position >> 1])

    def col(z, x):
        return (z * planes + x) * gy

    def edge(z, k):
        return (z * 2 + k) * gy

    def swap(array, mask, axis):
        count = lax.axis_size(axis)
        return lax.ppermute(array, axis, [(i, i ^ mask) for i in range(count)])

    ahead = [(i, (i + 1) % doms) for i in range(doms)]
    behind = [((i + 1) % doms, i) for i in range(doms)]

    scalars = jnp.stack(
        [jnp.tile(energies, perts), first_step.reshape(columns), second_step.reshape(columns)]
    )

    def flatten_body(source, early, placed, flat, *edges):
        def rows_step(p, carry):
            rows = pl.ds(pl.multiple_of(p * orbs, orbs), orbs)
            for x in range(planes):
                wide = source[rows, x].reshape(orbs, gz * gy)
                for z in range(gz):
                    value = wide[:, z * gy : (z + 1) * gy]
                    flat[rows, col(z, x) : col(z, x) + gy] = value
                    part, inner = divmod(z, part_z)
                    if x < 2:
                        at = edge(inner, x)
                        edges[2 * part][rows, at : at + gy] = value.astype(bf16)
                    if x >= planes - 2:
                        at = edge(inner, x - planes + 2)
                        edges[2 * part + 1][rows, at : at + gy] = value.astype(bf16)
            return carry

        lax.fori_loop(0, source.shape[0] // orbs, rows_step, 0)

    flat_response, *edges1 = run(
        flatten_body,
        [(response.reshape(columns, planes, gz, gy), "v"), (scalars, "a"), (where, "a")],
        [((columns, cells), f32)]
        + [((columns, part_edge), bf16)] * (2 * halo_parts),
        limit=8,
        name="flatten",
    )

    def halos_of(edges):
        received = []
        for part in range(halo_parts):
            low = lax.ppermute(edges[2 * part + 1], "dom", ahead)
            high = lax.ppermute(edges[2 * part], "dom", behind)
            received.append((low, high))
        return received

    halos1 = halos_of(edges1)


    def setup_body(occ, pot, pert, xc, occ_flat, pot_flat, pert_flat, xc_flat):
        for x in range(planes):
            wide = occ[:, x].reshape(orbs, gz * gy)
            for z in range(gz):
                cut = slice(col(z, x), col(z, x) + gy)
                occ_flat[:, cut] = wide[:, z * gy : (z + 1) * gy]
                pot_flat[0:1, cut] = pot[x, z : z + 1, :]
                xc_flat[0:1, cut] = xc[x, z : z + 1, :]
                for p in range(perts):
                    pert_flat[p, 0:1, cut] = pert[p, x, z : z + 1, :]

    flat_occupied, flat_potential, flat_perturbation, flat_xc = run(
        setup_body,
        [(occupied, "v"), (potential, "v"), (perturbation, "v"), (xc_kernel, "v")],
        [
            ((orbs, cells), f32),
            ((1, cells), f32),
            ((perts, 1, cells), f32),
            ((1, cells), f32),
        ],
        limit=2,
        name="setup",
    )

    chunk = min(256, locked)
    chunks = locked // chunk

    def relay_body(source, target, held, ready, in_sems, out_sems):
        def rows_of(i):
            return pl.ds(pl.multiple_of(i * chunk, chunk), chunk)

        def fetch(i):
            slot = lax.rem(i, 3)
            return pltpu.make_async_copy(source.at[rows_of(i)], held.at[slot], in_sems.at[slot])

        def flush(i):
            slot = lax.rem(i, 2)
            return pltpu.make_async_copy(ready.at[slot], target.at[rows_of(i)], out_sems.at[slot])

        fetch(0).start()
        fetch(1).start()

        def step(i, carry):
            @pl.when(i + 2 < chunks)
            def _():
                fetch(i + 2).start()

            @pl.when(i >= 2)
            def _():
                flush(i - 2).wait()

            fetch(i).wait()
            for x in range(planes):
                wide = held[lax.rem(i, 3), :, x].reshape(chunk, gz * gy)
                for z in range(gz):
                    ready[lax.rem(i, 2), :, col(z, x) : col(z, x) + gy] = wide[
                        :, z * gy : (z + 1) * gy
                    ]
            flush(i).start()
            return carry

        lax.fori_loop(0, chunks, step, 0)
        flush(chunks - 2).wait()
        flush(chunks - 1).wait()

    (locked_flat,) = run(
        relay_body,
        [(locked_set, "h")],
        [((locked, cells), bf16, "h")],
        scratch=[
            pltpu.VMEM((3, chunk, planes, gz, gy), bf16),
            pltpu.VMEM((2, chunk, cells), bf16),
            pltpu.SemaphoreType.DMA((3,)),
            pltpu.SemaphoreType.DMA((2,)),
        ],
        limit=12,
        name="relay",
    )

    def stencil_body(field, pot, scal, out, energy):
        energy[...] = per_row(scal, 0, gy)
        block = 32

        def rows_step(i, carry):
            rows = pl.ds(pl.multiple_of(i * block, block), block)
            base = energy[rows, :] + centre_half

            def at(z, x):
                return field[rows, col(z, x) : col(z, x) + gy]

            for z in range(gz):
                for x in range(planes):
                    here = at(z, x)
                    near = pltpu.roll(here, 1, 1) + pltpu.roll(here, gy - 1, 1)
                    far = pltpu.roll(here, 2, 1) + pltpu.roll(here, gy - 2, 1)
                    for d in (-1, 1):
                        if 0 <= x + d < planes:
                            near = near + at(z, x + d)
                        if 0 <= z + d < gz:
                            near = near + at(z + d, x)
                        if 0 <= x + 2 * d < planes:
                            far = far + at(z, x + 2 * d)
                        if 0 <= z + 2 * d < gz:
                            far = far + at(z + 2 * d, x)
                    own = base - pot[0:1, col(z, x) : col(z, x) + gy]
                    out[rows, col(z, x) : col(z, x) + gy] = (
                        own * here + near_half * near + far_half * far
                    )
            return carry

        lax.fori_loop(0, columns // block, rows_step, 0)

    def stencil(field):
        (out,) = run(
            stencil_body,
            [(field, "v"), (flat_potential, "v"), (scalars, "v")],
            [((columns, cells), f32)],
            scratch=[pltpu.VMEM((columns, gy), f32)],
            limit=1,
            name="stencil",
        )
        return out

    def finish_rhs(part, partial, low, high, occ, pot, rhs, rounded):
        first = part * part_z

        def rows_step(p, carry):
            rows = pl.ds(pl.multiple_of(p * orbs, orbs), orbs)
            for inner in range(part_z):
                for x in range(planes):
                    at = col(first + inner, x)
                    value = partial[rows, at : at + gy] - pot[p, 0:1, at : at + gy] * occ[
                        :, at : at + gy
                    ]

                    def halo(ref, k):
                        start = edge(inner, k)
                        return ref[rows, start : start + gy].astype(f32)

                    if x == 0:
                        value = value + (near_half * halo(low, 1) + far_half * halo(low, 0))
                    if x == 1:
                        value = value + far_half * halo(low, 1)
                    if x == planes - 2:
                        value = value + far_half * halo(high, 0)
                    if x == planes - 1:
                        value = value + (near_half * halo(high, 0) + far_half * halo(high, 1))
                    rhs[rows, at : at + gy] = value
                    rounded[rows, at : at + gy] = value.astype(bf16)
            return carry

        lax.fori_loop(0, perts, rows_step, 0)

    def margins(partial, halos, pot):
        low, high = halos[0]

        def piece_copies(where_ref, start, lock, buf, sems):
            copies = []
            for m in range(chips):
                rows = pl.ds(pl.multiple_of(start + (where_ref[1] ^ m) * piece, piece), piece)
                copies.append(pltpu.make_async_copy(lock.at[rows], buf.at[m], sems.at[m]))
            return copies

        piece_scratch = [pltpu.VMEM((chips, piece, cells), bf16), pltpu.SemaphoreType.DMA((chips,))]

        def other_body(
            where_ref, part_ref, low_ref, high_ref, occ, pot_ref, lock, rhs, rounded, out, buf, sems
        ):
            copies = piece_copies(where_ref, (1 - where_ref[0]) * half, lock, buf, sems)
            for copy in copies:
                copy.start()
            finish_rhs(0, part_ref, low_ref, high_ref, occ, pot_ref, rhs, rounded)
            for m in range(chips):
                copies[m].wait()
                out[:, m * piece : (m + 1) * piece] = dot_nt(rounded[...], buf[m]).astype(bf16)

        rhs, rounded, other = run(
            other_body,
            [
                (where, "s"),
                (partial, "v"),
                (low, "v"),
                (high, "v"),
                (flat_occupied, "v"),
                (pot, "v"),
                (locked_flat, "h"),
            ],
            [((columns, cells), f32), ((columns, cells), bf16), ((columns, half), bf16)],
            scratch=piece_scratch,
            aliases={1: 0},
            limit=20,
            name="margin_other",
        )
        arrived = swap(other, 1, "dom")

        def own_body(where_ref, rounded_ref, lock, out, buf, sems):
            copies = piece_copies(where_ref, where_ref[0] * half, lock, buf, sems)
            for copy in copies:
                copy.start()
            for m in range(chips):
                copies[m].wait()
                out[:, m * piece : (m + 1) * piece] = dot_nt(rounded_ref[...], buf[m])

        (own,) = run(
            own_body,
            [(where, "s"), (rounded, "v"), (locked_flat, "h")],
            [((columns, half), f32)],
            scratch=piece_scratch,
            limit=20,
            name="margin_own",
        )

        def pair_body(own_ref, arrived_ref, kept, *sent):
            for m in range(chips):
                cut = slice(m * piece, (m + 1) * piece)
                value = own_ref[:, cut] + arrived_ref[:, cut].astype(f32)
                if m == 0:
                    kept[...] = value
                else:
                    sent[m - 1][...] = value.astype(bf16)

        kept, *sent = run(
            pair_body,
            [(own, "v"), (arrived, "v")],
            [((columns, piece), f32)] + [((columns, piece), bf16)] * (chips - 1),
            limit=6,
            name="margin_pair",
        )
        arrivals = [swap(sent[m - 1], 2 * m, "dom") for m in range(1, chips)]

        def add_body(*refs):
            out = refs[-1]
            out[...] = tree_sum([r[...].astype(f32) for r in refs[:-1]]).astype(bf16)

        (mine,) = run(
            add_body,
            [(kept, "v")] + [(r, "v") for r in arrivals],
            [((columns, piece), bf16)],
            limit=2,
            name="add_pieces",
        )
        gathered = [mine] + [swap(mine, 2 * m, "dom") for m in range(1, chips)]
        return rhs, gathered

    def collect(where_ref, pieces, held):
        for m, ref in enumerate(pieces):
            at = pl.ds(pl.multiple_of((where_ref[1] ^ m) * piece, piece), piece)
            held[:, at] = ref[...]

    stripe_scratch = [pltpu.VMEM((gz, half, stripe), bf16), pltpu.SemaphoreType.DMA((gz,))]

    def stripe_copy(start, lock, buf, sems, z):
        rows = pl.ds(pl.multiple_of(start, half), half)
        at = pl.ds(pl.multiple_of(z * stripe, stripe), stripe)
        return pltpu.make_async_copy(lock.at[rows, at], buf.at[z], sems.at[z])

    def remove_own(gathered):
        def body(where_ref, *refs):
            pieces, (lock, acc, held, buf, sems) = refs[:chips], refs[chips:]
            start = where_ref[0] * half
            for z in range(gz):
                stripe_copy(start, lock, buf, sems, z).start()
            collect(where_ref, pieces, held)

            def step(z, carry):
                at = pl.ds(pl.multiple_of(z * stripe, stripe), stripe)
                stripe_copy(start, lock, buf, sems, z).wait()
                acc[:, at] = dot_nn(held[...], buf[z])
                return carry

            lax.fori_loop(0, gz, step, 0)

        (acc,) = run(
            body,
            [(where, "s")] + [(g, "v") for g in gathered] + [(locked_flat, "h")],
            [((columns, cells), f32)],
            scratch=[pltpu.VMEM((columns, half), bf16)] + stripe_scratch,
            limit=22,
            name="remove_own",
        )
        return acc

    def line_of(lanes):
        return jnp.sum(lanes.T, axis=0, keepdims=True)

    def squares(value):
        total = value[:, :gy] * value[:, :gy]
        for x in range(1, planes):
            total = total + value[:, x * gy : (x + 1) * gy] * value[:, x * gy : (x + 1) * gy]
        return total

    def first_finish(others, acc, rhs, field):
        def body(where_ref, *refs):
            pieces = refs[:chips]
            lock, acc_ref, rhs_ref, field_ref, occ, scal = refs[chips : chips + 6]
            res, mid, low, high, dens, norm = refs[chips + 6 : chips + 12]
            held, step_rows, lanes, buf, sems = refs[chips + 12 :]
            start = (1 - where_ref[0]) * half
            for z in range(gz):
                stripe_copy(start, lock, buf, sems, z).start()
            collect(where_ref, pieces, held)
            step_rows[...] = per_row(scal, 1, gy)
            lanes[...] = jnp.zeros_like(lanes)

            def step(z, carry):
                at = pl.ds(pl.multiple_of(z * stripe, stripe), stripe)
                stripe_copy(start, lock, buf, sems, z).wait()
                removed = acc_ref[:, at] + dot_nn(held[...], buf[z])
                value = rhs_ref[:, at] - removed
                res[:, at] = value
                lanes[...] += squares(value)
                for x in range(planes):
                    cut = slice(x * gy, (x + 1) * gy)
                    spot = pl.ds(pl.multiple_of(z * stripe + x * gy, gy), gy)
                    new = field_ref[:, spot] + step_rows[...] * value[:, cut]
                    mid[:, spot] = new
                    weight = 2.0 * occ[:, spot]
                    sums = [
                        jnp.sum(weight * new[p * orbs : (p + 1) * orbs], axis=0, keepdims=True)
                        for p in range(perts)
                    ]
                    dens[:, spot] = jnp.concatenate(sums, axis=0).astype(bf16)
                    if x < 2:
                        place = pl.ds(pl.multiple_of((z * 2 + x) * gy, gy), gy)
                        low[:, place] = new.astype(bf16)
                    if x >= planes - 2:
                        place = pl.ds(pl.multiple_of((z * 2 + x - planes + 2) * gy, gy), gy)
                        high[:, place] = new.astype(bf16)
                return carry

            lax.fori_loop(0, gz, step, 0)
            norm[...] = line_of(lanes[...])

        return run(
            body,
            [(where, "s")]
            + [(g, "v") for g in others]
            + [
                (locked_flat, "h"),
                (acc, "v"),
                (rhs, "v"),
                (field, "v"),
                (flat_occupied, "v"),
                (scalars, "v"),
            ],
            [
                ((columns, cells), f32),
                ((columns, cells), f32),
                ((columns, gz * 2 * gy), bf16),
                ((columns, gz * 2 * gy), bf16),
                ((perts, cells), bf16),
                ((1, columns), f32),
            ],
            scratch=[
                pltpu.VMEM((columns, half), bf16),
                pltpu.VMEM((columns, gy), f32),
                pltpu.VMEM((columns, gy), f32),
            ]
            + stripe_scratch,
            aliases={chips + 3: 0, chips + 4: 1},
            limit=26,
            name="first_finish",
        )

    def second_finish(others, acc, rhs, before):
        def body(where_ref, *refs):
            pieces = refs[:chips]
            lock, acc_ref, rhs_ref, first, res, norm, held, lanes, buf, sems = refs[chips:]
            start = (1 - where_ref[0]) * half
            for z in range(gz):
                stripe_copy(start, lock, buf, sems, z).start()
            collect(where_ref, pieces, held)
            lanes[...] = jnp.zeros_like(lanes)

            def step(z, carry):
                at = pl.ds(pl.multiple_of(z * stripe, stripe), stripe)
                stripe_copy(start, lock, buf, sems, z).wait()
                removed = acc_ref[:, at] + dot_nn(held[...], buf[z])
                value = rhs_ref[:, at] - removed
                res[:, at] = value
                lanes[...] += squares(value)
                return carry

            lax.fori_loop(0, gz, step, 0)
            norm[0:1, :] = first[...]
            norm[1:2, :] = line_of(lanes[...])

        return run(
            body,
            [(where, "s")]
            + [(g, "v") for g in others]
            + [(locked_flat, "h"), (acc, "v"), (rhs, "v"), (before, "v")],
            [((columns, cells), f32), ((2, columns), f32)],
            scratch=[pltpu.VMEM((columns, half), bf16), pltpu.VMEM((columns, gy), f32)]
            + stripe_scratch,
            aliases={chips + 3: 0},
            limit=22,
            name="second_finish",
        )

    def across(array, axis):
        return [array] + [swap(array, m, axis) for m in range(1, lax.axis_size(axis))]

    partial1 = stencil(flat_response)
    rhs1, gathered1 = margins(partial1, halos1, flat_perturbation)
    others1 = [swap(g, 1, "dom") for g in gathered1]
    acc1 = remove_own(gathered1)
    first_res, middle, low_edge, high_edge, dens, norm1 = first_finish(
        others1, acc1, rhs1, flat_response
    )
    halos2 = halos_of([low_edge, high_edge])
    densities = across(dens, "band")

    def potential_body(*refs):
        parts = refs[:bands]
        pert, xc, flat, native = refs[bands:]
        density = tree_sum([r[...].astype(f32) for r in parts])
        for z in range(gz):
            for x in range(planes):
                cut = slice(col(z, x), col(z, x) + gy)
                for p in range(perts):
                    value = pert[p, 0:1, cut] - xc[0:1, cut] * density[p : p + 1, cut]
                    flat[p, 0:1, cut] = value
                    native[p, x, z : z + 1, :] = value

    flat_rp, response_potential = run(
        potential_body,
        [(d, "v") for d in densities]
        + [(flat_perturbation, "v"), (flat_xc, "v")],
        [
            ((perts, 1, cells), f32),
            ((perts, planes, gz, gy), f32),
        ],
        limit=3,
        name="potential",
    )

    partial2 = stencil(middle)
    rhs2, gathered2 = margins(partial2, halos2, flat_rp)
    others2 = [swap(g, 1, "dom") for g in gathered2]
    acc2 = remove_own(gathered2)
    second_res, norms = second_finish(others2, acc2, rhs2, norm1)
    other_norms = swap(norms, 1, "dom")

    def norm_body(one, two, out):
        out[...] = one[...] + two[...]

    (pair_norms,) = run(
        norm_body,
        [(norms, "v"), (other_norms, "v")],
        [((2, columns), f32)],
        limit=1,
        name="norm_pair",
    )
    all_norms = [pair_norms] + [swap(pair_norms, 2 * m, "dom") for m in range(1, chips)]

    def final_body(*refs):
        sums = tree_sum([r[...] for r in refs[:chips]])
        mid, res1, res2, scal, out, steps, blends = refs[chips:]
        ratio = sums[1:2, :] / sums[0:1, :]
        blend = scal[2:3, :] * ratio
        steps[...] = per_row(scal, 2, gy)
        blends[...] = jnp.broadcast_to(blend, (gy, columns)).T
        block = 64 if columns % 64 == 0 else columns

        def rows_step(i, carry):
            rows = pl.ds(pl.multiple_of(i * block, block), block)
            step, mix = steps[rows, :], blends[rows, :]
            for x in range(planes):
                values = []
                for z in range(gz):
                    cut = slice(col(z, x), col(z, x) + gy)
                    values.append(mid[rows, cut] + step * res2[rows, cut] + mix * res1[rows, cut])
                out[rows, x] = jnp.concatenate(values, axis=1).reshape(block, gz, gy)
            return carry

        lax.fori_loop(0, columns // block, rows_step, 0)

    (new_response,) = run(
        final_body,
        [(n, "v") for n in all_norms]
        + [(middle, "v"), (first_res, "v"), (second_res, "v"), (scalars, "v")],
        [((columns, planes, gz, gy), f32)],
        scratch=[pltpu.VMEM((columns, gy), f32), pltpu.VMEM((columns, gy), f32)],
        limit=5,
        name="final",
    )
    return new_response.reshape(response.shape), response_potential


def solution(mesh):
    placed = (
        P(None, "band", "dom", None, None),
        P("band", "dom", None, None),
        P(None, "dom", None, None),
        P("dom", None, None),
        P(None, "dom", None, None),
        P("dom", None, None),
        P("band"),
        P(None, "band"),
        P(None, "band"),
    )
    return jax.shard_map(
        local,
        mesh=mesh,
        in_specs=placed,
        out_specs=(P(None, "band", "dom", None, None), P(None, "dom", None, None)),
        check_vma=False,
    )
```

```python
import jax
import jax.numpy as jnp
from jax import lax
from jax.experimental import pallas as pl
from jax.experimental.pallas import tpu as pltpu
from jax.sharding import PartitionSpec as P

f32 = jnp.float32
bf16 = jnp.bfloat16
near_half = 2.0 / 3.0
far_half = -1.0 / 24.0
centre_half = -3.75
MIB = 1 << 20


def run(body, args, outs, scratch=(), aliases=None, limit=8, name=None):
    kinds = {"v": pltpu.VMEM, "s": pltpu.SMEM, "a": pl.ANY, "h": pltpu.HBM}
    results = pl.pallas_call(
        body,
        in_specs=[pl.BlockSpec(memory_space=kinds[kind]) for _, kind in args],
        out_specs=[pl.BlockSpec(memory_space=kinds[out[2] if len(out) > 2 else "v"]) for out in outs],
        out_shape=[
            pltpu.HBM(out[0], out[1]) if out[2:] == ("h",) else jax.ShapeDtypeStruct(out[0], out[1])
            for out in outs
        ],
        scratch_shapes=list(scratch),
        input_output_aliases=aliases or {},
        compiler_params=pltpu.CompilerParams(vmem_limit_bytes=limit * MIB),
        name=name,
    )(*[array for array, _ in args])
    return list(results)


def tree_sum(terms):
    while len(terms) > 1:
        terms = [terms[i] + terms[i + 1] for i in range(0, len(terms), 2)]
    return terms[0]


def per_row(scalars, row, width):
    line = scalars[row : row + 1, :]
    return jnp.broadcast_to(line, (width, line.shape[1])).T


def dot_nt(a, b):
    return lax.dot_general(a, b, (((1,), (1,)), ((), ())), preferred_element_type=f32)


def dot_nn(a, b):
    return lax.dot_general(a, b, (((1,), (0,)), ((), ())), preferred_element_type=f32)


def local(
    response,
    occupied,
    locked_set,
    potential,
    perturbation,
    xc_kernel,
    energies,
    first_step,
    second_step,
):
    perts, orbs, planes, gz, gy = response.shape
    locked = locked_set.shape[0]
    columns = perts * orbs
    cells = planes * gz * gy
    stripe = planes * gy
    doms = lax.axis_size("dom")
    bands = lax.axis_size("band")
    chips = doms // 2
    half = locked // 2
    piece = half // chips
    part_z = gz // 2
    part_cells = part_z * stripe
    part_edge = part_z * 2 * gy
    position = lax.axis_index("dom")
    where = jnp.stack([position & 1, position >> 1])

    def col(z, x):
        return (z * planes + x) * gy

    def edge(z, k):
        return (z * 2 + k) * gy

    def swap(array, mask, axis):
        count = lax.axis_size(axis)
        return lax.ppermute(array, axis, [(i, i ^ mask) for i in range(count)])

    ahead = [(i, (i + 1) % doms) for i in range(doms)]
    behind = [((i + 1) % doms, i) for i in range(doms)]

    scalars = jnp.stack(
        [jnp.tile(energies, perts), first_step.reshape(columns), second_step.reshape(columns)]
    )

    def flatten_body(source, early, placed, flat, *edges):
        def rows_step(p, carry):
            rows = pl.ds(pl.multiple_of(p * orbs, orbs), orbs)
            for x in range(planes):
                wide = source[rows, x].reshape(orbs, gz * gy)
                for z in range(gz):
                    value = wide[:, z * gy : (z + 1) * gy]
                    flat[rows, col(z, x) : col(z, x) + gy] = value
                    if x < 2:
                        at = edge(z, x)
                        edges[0][rows, at : at + gy] = value.astype(bf16)
                    if x >= planes - 2:
                        at = edge(z, x - planes + 2)
                        edges[1][rows, at : at + gy] = value.astype(bf16)
            return carry

        lax.fori_loop(0, source.shape[0] // orbs, rows_step, 0)

    flat_response, *edges1 = run(
        flatten_body,
        [(response.reshape(columns, planes, gz, gy), "v"), (scalars, "a"), (where, "a")],
        [((columns, cells), f32)]
        + [((columns, gz * 2 * gy), bf16)] * 2,
        limit=8,
        name="flatten",
    )

    def halos_of(low_edge, high_edge):
        return lax.ppermute(high_edge, "dom", ahead), lax.ppermute(low_edge, "dom", behind)

    halos1 = halos_of(*edges1)


    def setup_body(occ, pot, pert, xc, occ_flat, pot_flat, pert_flat, xc_flat):
        for x in range(planes):
            wide = occ[:, x].reshape(orbs, gz * gy)
            for z in range(gz):
                cut = slice(col(z, x), col(z, x) + gy)
                occ_flat[:, cut] = wide[:, z * gy : (z + 1) * gy]
                pot_flat[0:1, cut] = pot[x, z : z + 1, :]
                xc_flat[0:1, cut] = xc[x, z : z + 1, :]
                for p in range(perts):
                    pert_flat[p, 0:1, cut] = pert[p, x, z : z + 1, :]

    flat_occupied, flat_potential, flat_perturbation, flat_xc = run(
        setup_body,
        [(occupied, "v"), (potential, "v"), (perturbation, "v"), (xc_kernel, "v")],
        [
            ((orbs, cells), f32),
            ((1, cells), f32),
            ((perts, 1, cells), f32),
            ((1, cells), f32),
        ],
        limit=2,
        name="setup",
    )

    chunk = min(256, locked)
    chunks = locked // chunk

    def relay_body(source, target, held, ready, in_sems, out_sems):
        def rows_of(i):
            return pl.ds(pl.multiple_of(i * chunk, chunk), chunk)

        def fetch(i):
            slot = lax.rem(i, 3)
            return pltpu.make_async_copy(source.at[rows_of(i)], held.at[slot], in_sems.at[slot])

        def flush(i):
            slot = lax.rem(i, 2)
            return pltpu.make_async_copy(ready.at[slot], target.at[rows_of(i)], out_sems.at[slot])

        fetch(0).start()
        fetch(1).start()

        def step(i, carry):
            @pl.when(i + 2 < chunks)
            def _():
                fetch(i + 2).start()

            @pl.when(i >= 2)
            def _():
                flush(i - 2).wait()

            fetch(i).wait()
            for x in range(planes):
                wide = held[lax.rem(i, 3), :, x].reshape(chunk, gz * gy)
                for z in range(gz):
                    ready[lax.rem(i, 2), :, col(z, x) : col(z, x) + gy] = wide[
                        :, z * gy : (z + 1) * gy
                    ]
            flush(i).start()
            return carry

        lax.fori_loop(0, chunks, step, 0)
        flush(chunks - 2).wait()
        flush(chunks - 1).wait()

    (locked_flat,) = run(
        relay_body,
        [(pltpu.with_memory_space_constraint(locked_set, pltpu.HBM), "h")],
        [((locked, cells), bf16, "h")],
        scratch=[
            pltpu.VMEM((3, chunk, planes, gz, gy), bf16),
            pltpu.VMEM((2, chunk, cells), bf16),
            pltpu.SemaphoreType.DMA((3,)),
            pltpu.SemaphoreType.DMA((2,)),
        ],
        limit=12,
        name="relay",
    )

    locked_flat = pltpu.with_memory_space_constraint(locked_flat, pltpu.HBM)

    def stencil_body(field, pot, scal, out, energy):
        energy[...] = per_row(scal, 0, gy)
        block = 32

        def rows_step(i, carry):
            rows = pl.ds(pl.multiple_of(i * block, block), block)
            base = energy[rows, :] + centre_half

            def at(z, x):
                return field[rows, col(z, x) : col(z, x) + gy]

            for z in range(gz):
                for x in range(planes):
                    here = at(z, x)
                    near = pltpu.roll(here, 1, 1) + pltpu.roll(here, gy - 1, 1)
                    far = pltpu.roll(here, 2, 1) + pltpu.roll(here, gy - 2, 1)
                    for d in (-1, 1):
                        if 0 <= x + d < planes:
                            near = near + at(z, x + d)
                        if 0 <= z + d < gz:
                            near = near + at(z + d, x)
                        if 0 <= x + 2 * d < planes:
                            far = far + at(z, x + 2 * d)
                        if 0 <= z + 2 * d < gz:
                            far = far + at(z + 2 * d, x)
                    own = base - pot[0:1, col(z, x) : col(z, x) + gy]
                    out[rows, col(z, x) : col(z, x) + gy] = (
                        own * here + near_half * near + far_half * far
                    )
            return carry

        lax.fori_loop(0, columns // block, rows_step, 0)

    def stencil(field):
        (out,) = run(
            stencil_body,
            [(field, "v"), (flat_potential, "v"), (scalars, "v")],
            [((columns, cells), f32)],
            scratch=[pltpu.VMEM((columns, gy), f32)],
            limit=1,
            name="stencil",
        )
        return out

    def finish_rhs(first, count, partial, low, high, occ, pot, rhs, rounded):

        def rows_step(p, carry):
            rows = pl.ds(pl.multiple_of(p * orbs, orbs), orbs)
            for inner in range(count):
                for x in range(planes):
                    at = col(first + inner, x)
                    spot = col(inner, x)
                    value = partial[rows, at : at + gy] - pot[p, 0:1, spot : spot + gy] * occ[
                        :, at : at + gy
                    ]

                    def halo(ref, k):
                        start = edge(inner, k)
                        return ref[rows, start : start + gy].astype(f32)

                    if x == 0:
                        value = value + (near_half * halo(low, 1) + far_half * halo(low, 0))
                    if x == 1:
                        value = value + far_half * halo(low, 1)
                    if x == planes - 2:
                        value = value + far_half * halo(high, 0)
                    if x == planes - 1:
                        value = value + (near_half * halo(high, 0) + far_half * halo(high, 1))
                    rhs[rows, at : at + gy] = value
                    rounded[rows, spot : spot + gy] = value.astype(bf16)
            return carry

        lax.fori_loop(0, perts, rows_step, 0)

    def reduce_pieces(own, arrived):
        def pair_body(own_ref, arrived_ref, kept, *sent):
            for m in range(chips):
                cut = slice(m * piece, (m + 1) * piece)
                value = own_ref[:, cut] + arrived_ref[:, cut].astype(f32)
                if m == 0:
                    kept[...] = value
                else:
                    sent[m - 1][...] = value.astype(bf16)

        kept, *sent = run(
            pair_body,
            [(own, "v"), (arrived, "v")],
            [((columns, piece), f32)] + [((columns, piece), bf16)] * (chips - 1),
            limit=6,
            name="margin_pair",
        )
        arrivals = [swap(sent[m - 1], 2 * m, "dom") for m in range(1, chips)]

        def add_body(*refs):
            out = refs[-1]
            out[...] = tree_sum([r[...].astype(f32) for r in refs[:-1]]).astype(bf16)

        (mine,) = run(
            add_body,
            [(kept, "v")] + [(r, "v") for r in arrivals],
            [((columns, piece), bf16)],
            limit=2,
            name="add_pieces",
        )
        gathered = [mine] + [swap(mine, 2 * m, "dom") for m in range(1, chips)]
        return gathered

    def margins_in_parts(partial, halos, pot):
        def column_copies(where_ref, both, first, lock, buf, sems):
            copies = []
            for k in range(len(both)):
                start = (where_ref[0] ^ both[k]) * half
                for m in range(chips):
                    rows = pl.ds(pl.multiple_of(start + (where_ref[1] ^ m) * piece, piece), piece)
                    index = k * chips + m
                    copies.append(
                        pltpu.make_async_copy(
                            lock.at[rows, first * part_cells : (first + 1) * part_cells],
                            buf.at[index],
                            sems.at[index],
                        )
                    )
            return copies

        def scratch_of(count):
            return [
                pltpu.VMEM((count, piece, part_cells), bf16),
                pltpu.SemaphoreType.DMA((count,)),
            ]

        def early_body(where_ref, part_ref, low, high, occ, pot_ref, lock, rhs, out, rounded, buf, sems):
            copies = column_copies(where_ref, (1, 0), 0, lock, buf, sems)
            for copy in copies:
                copy.start()
            finish_rhs(0, part_z, part_ref, low, high, occ, pot_ref, rhs, rounded)
            for m in range(2 * chips):
                copies[m].wait()
                out[:, m * piece : (m + 1) * piece] = dot_nt(rounded[...], buf[m])

        rhs, early = run(
            early_body,
            [
                (where, "s"),
                (partial, "v"),
                (halos[0][0], "v"),
                (halos[0][1], "v"),
                (flat_occupied, "v"),
                (pot[0], "v"),
                (locked_flat, "h"),
            ],
            [((columns, cells), f32), ((columns, locked), f32)],
            scratch=[pltpu.VMEM((columns, part_cells), bf16)] + scratch_of(2 * chips),
            aliases={1: 0},
            limit=24,
            name="margin_early",
        )

        def late_body(
            where_ref, part_ref, low, high, occ, pot_ref, lock, early_ref, rhs, rounded, out, buf, sems
        ):
            copies = column_copies(where_ref, (1,), 1, lock, buf, sems)
            for copy in copies:
                copy.start()
            finish_rhs(part_z, part_z, part_ref, low, high, occ, pot_ref, rhs, rounded)
            for m in range(chips):
                cut = slice(m * piece, (m + 1) * piece)
                copies[m].wait()
                out[:, cut] = (early_ref[:, cut] + dot_nt(rounded[...], buf[m])).astype(bf16)

        rhs, rounded, other = run(
            late_body,
            [
                (where, "s"),
                (rhs, "v"),
                (halos[1][0], "v"),
                (halos[1][1], "v"),
                (flat_occupied, "v"),
                (pot[1], "v"),
                (locked_flat, "h"),
                (early, "v"),
            ],
            [((columns, cells), f32), ((columns, part_cells), bf16), ((columns, half), bf16)],
            scratch=scratch_of(chips),
            aliases={1: 0},
            limit=14,
            name="margin_late",
        )
        arrived = swap(other, 1, "dom")

        def own_body(where_ref, rounded_ref, lock, early_ref, out, buf, sems):
            copies = column_copies(where_ref, (0,), 1, lock, buf, sems)
            for copy in copies:
                copy.start()
            for m in range(chips):
                cut = slice(m * piece, (m + 1) * piece)
                old = early_ref[:, half + m * piece : half + (m + 1) * piece]
                copies[m].wait()
                out[:, cut] = old + dot_nt(rounded_ref[...], buf[m])

        (own,) = run(
            own_body,
            [(where, "s"), (rounded, "v"), (locked_flat, "h"), (early, "v")],
            [((columns, half), f32)],
            scratch=scratch_of(chips),
            limit=14,
            name="margin_late_own",
        )
        return rhs, reduce_pieces(own, arrived)

    def margins(partial, halos, pot):
        low, high = halos

        def piece_copies(where_ref, start, lock, buf, sems):
            copies = []
            for m in range(chips):
                rows = pl.ds(pl.multiple_of(start + (where_ref[1] ^ m) * piece, piece), piece)
                copies.append(pltpu.make_async_copy(lock.at[rows], buf.at[m], sems.at[m]))
            return copies

        piece_scratch = [pltpu.VMEM((chips, piece, cells), bf16), pltpu.SemaphoreType.DMA((chips,))]

        def other_body(
            where_ref, part_ref, low_ref, high_ref, occ, pot_ref, lock, rhs, rounded, out, buf, sems
        ):
            copies = piece_copies(where_ref, (1 - where_ref[0]) * half, lock, buf, sems)
            for copy in copies:
                copy.start()
            finish_rhs(0, gz, part_ref, low_ref, high_ref, occ, pot_ref, rhs, rounded)
            for m in range(chips):
                copies[m].wait()
                out[:, m * piece : (m + 1) * piece] = dot_nt(rounded[...], buf[m]).astype(bf16)

        rhs, rounded, other = run(
            other_body,
            [
                (where, "s"),
                (partial, "v"),
                (low, "v"),
                (high, "v"),
                (flat_occupied, "v"),
                (pot, "v"),
                (locked_flat, "h"),
            ],
            [((columns, cells), f32), ((columns, cells), bf16), ((columns, half), bf16)],
            scratch=piece_scratch,
            aliases={1: 0},
            limit=20,
            name="margin_other",
        )
        arrived = swap(other, 1, "dom")

        def own_body(where_ref, rounded_ref, lock, out, buf, sems):
            copies = piece_copies(where_ref, where_ref[0] * half, lock, buf, sems)
            for copy in copies:
                copy.start()
            for m in range(chips):
                copies[m].wait()
                out[:, m * piece : (m + 1) * piece] = dot_nt(rounded_ref[...], buf[m])

        (own,) = run(
            own_body,
            [(where, "s"), (rounded, "v"), (locked_flat, "h")],
            [((columns, half), f32)],
            scratch=piece_scratch,
            limit=20,
            name="margin_own",
        )

        return rhs, reduce_pieces(own, arrived)

    def collect(where_ref, pieces, held):
        for m, ref in enumerate(pieces):
            at = pl.ds(pl.multiple_of((where_ref[1] ^ m) * piece, piece), piece)
            held[:, at] = ref[...]

    stripe_scratch = [pltpu.VMEM((gz, half, stripe), bf16), pltpu.SemaphoreType.DMA((gz,))]

    def stripe_copy(start, lock, buf, sems, z):
        rows = pl.ds(pl.multiple_of(start, half), half)
        at = pl.ds(pl.multiple_of(z * stripe, stripe), stripe)
        return pltpu.make_async_copy(lock.at[rows, at], buf.at[z], sems.at[z])

    def remove_own(gathered):
        def body(where_ref, *refs):
            pieces, (lock, acc, held, buf, sems) = refs[:chips], refs[chips:]
            start = where_ref[0] * half
            for z in range(gz):
                stripe_copy(start, lock, buf, sems, z).start()
            collect(where_ref, pieces, held)

            def step(z, carry):
                at = pl.ds(pl.multiple_of(z * stripe, stripe), stripe)
                stripe_copy(start, lock, buf, sems, z).wait()
                acc[:, at] = dot_nn(held[...], buf[z])
                return carry

            lax.fori_loop(0, gz, step, 0)

        (acc,) = run(
            body,
            [(where, "s")] + [(g, "v") for g in gathered] + [(locked_flat, "h")],
            [((columns, cells), f32)],
            scratch=[pltpu.VMEM((columns, half), bf16)] + stripe_scratch,
            limit=22,
            name="remove_own",
        )
        return acc

    def line_of(lanes):
        return jnp.sum(lanes.T, axis=0, keepdims=True)

    def squares(value):
        total = value[:, :gy] * value[:, :gy]
        for x in range(1, planes):
            total = total + value[:, x * gy : (x + 1) * gy] * value[:, x * gy : (x + 1) * gy]
        return total

    def first_finish(part, others, acc, rhs, field, before):
        extra = [(array, "v") for array in before]
        base = part * part_z
        origin = 0 if part else base
        width = part_cells * (part + 1)

        def body(where_ref, *refs):
            pieces = refs[:chips]
            lock, acc_ref, rhs_ref, field_ref, occ, scal = refs[chips : chips + 6]
            rest = refs[chips + 6 :]
            old, rest = rest[: len(extra)], rest[len(extra) :]
            res, mid, low, high, dens, norm, held, step_rows, lanes, buf, sems = rest
            start = (1 - where_ref[0]) * half
            for z in range(base, base + part_z):
                stripe_copy(start, lock, buf, sems, z).start()
            collect(where_ref, pieces, held)
            step_rows[...] = per_row(scal, 1, gy)
            lanes[...] = jnp.zeros_like(lanes)

            def step(z, carry):
                at = pl.ds(pl.multiple_of(z * stripe, stripe), stripe)
                stripe_copy(start, lock, buf, sems, z).wait()
                removed = acc_ref[:, at] + dot_nn(held[...], buf[z])
                value = rhs_ref[:, at] - removed
                res[:, at] = value
                lanes[...] += squares(value)
                for x in range(planes):
                    cut = slice(x * gy, (x + 1) * gy)
                    spot = pl.ds(pl.multiple_of(z * stripe + x * gy, gy), gy)
                    new = field_ref[:, spot] + step_rows[...] * value[:, cut]
                    mid[:, spot] = new
                    weight = 2.0 * occ[:, spot]
                    sums = [
                        jnp.sum(weight * new[p * orbs : (p + 1) * orbs], axis=0, keepdims=True)
                        for p in range(perts)
                    ]
                    kept = pl.ds(pl.multiple_of((z - origin) * stripe + x * gy, gy), gy)
                    dens[:, kept] = jnp.concatenate(sums, axis=0).astype(bf16)
                    if x < 2:
                        place = pl.ds(pl.multiple_of(((z - base) * 2 + x) * gy, gy), gy)
                        low[:, place] = new.astype(bf16)
                    if x >= planes - 2:
                        place = pl.ds(pl.multiple_of(((z - base) * 2 + x - planes + 2) * gy, gy), gy)
                        high[:, place] = new.astype(bf16)
                return carry

            lax.fori_loop(base, base + part_z, step, 0)
            norm[...] = line_of(lanes[...])
            if old:
                norm[...] += old[1][...]
                dens[:, :part_cells] = old[0][...]

        return run(
            body,
            [(where, "s")]
            + [(g, "v") for g in others]
            + [
                (locked_flat, "h"),
                (acc, "v"),
                (rhs, "v"),
                (field, "v"),
                (flat_occupied, "v"),
                (scalars, "v"),
            ]
            + extra,
            [
                ((columns, cells), f32),
                ((columns, cells), f32),
                ((columns, part_edge), bf16),
                ((columns, part_edge), bf16),
                ((perts, width), bf16),
                ((1, columns), f32),
            ],
            scratch=[
                pltpu.VMEM((columns, half), bf16),
                pltpu.VMEM((columns, gy), f32),
                pltpu.VMEM((columns, gy), f32),
            ]
            + stripe_scratch,
            aliases={chips + 3: 0, chips + 4: 1},
            limit=26,
            name="first_finish",
        )

    def second_finish(others, acc, rhs, before):
        def body(where_ref, *refs):
            pieces = refs[:chips]
            lock, acc_ref, rhs_ref, first, res, norm, held, lanes, buf, sems = refs[chips:]
            start = (1 - where_ref[0]) * half
            for z in range(gz):
                stripe_copy(start, lock, buf, sems, z).start()
            collect(where_ref, pieces, held)
            lanes[...] = jnp.zeros_like(lanes)

            def step(z, carry):
                at = pl.ds(pl.multiple_of(z * stripe, stripe), stripe)
                stripe_copy(start, lock, buf, sems, z).wait()
                removed = acc_ref[:, at] + dot_nn(held[...], buf[z])
                value = rhs_ref[:, at] - removed
                res[:, at] = value
                lanes[...] += squares(value)
                return carry

            lax.fori_loop(0, gz, step, 0)
            norm[0:1, :] = first[...]
            norm[1:2, :] = line_of(lanes[...])

        return run(
            body,
            [(where, "s")]
            + [(g, "v") for g in others]
            + [(locked_flat, "h"), (acc, "v"), (rhs, "v"), (before, "v")],
            [((columns, cells), f32), ((2, columns), f32)],
            scratch=[pltpu.VMEM((columns, half), bf16), pltpu.VMEM((columns, gy), f32)]
            + stripe_scratch,
            aliases={chips + 3: 0},
            limit=22,
            name="second_finish",
        )

    partial1 = stencil(flat_response)
    rhs1, gathered1 = margins(partial1, halos1, flat_perturbation)
    others1 = [swap(g, 1, "dom") for g in gathered1]
    acc1 = remove_own(gathered1)
    def add_body(one, two, out):
        out[...] = (one[...].astype(f32) + two[...].astype(f32)).astype(bf16)

    def potential_body(one, two, pert, xc, low, high, native):
        density = one[...].astype(f32) + two[...].astype(f32)
        for z in range(gz):
            for x in range(planes):
                cut = slice(col(z, x), col(z, x) + gy)
                spot = slice(col(z % part_z, x), col(z % part_z, x) + gy)
                flat = low if z < part_z else high
                for p in range(perts):
                    value = pert[p, 0:1, cut] - xc[0:1, cut] * density[p : p + 1, cut]
                    flat[p, 0:1, spot] = value
                    native[p, x, z : z + 1, :] = value

    halos2 = []
    first_res, middle, before = rhs1, flat_response, []
    for part in range(2):
        first_res, middle, low_edge, high_edge, dens, norm1 = first_finish(
            part, others1, acc1, first_res, middle, before
        )
        before = [dens, norm1]
        halos2.append(halos_of(low_edge, high_edge))
    mask = 1
    while 2 * mask < bands:
        (dens,) = run(
            add_body,
            [(dens, "v"), (swap(dens, mask, "band"), "v")],
            [((perts, cells), bf16)],
            limit=2,
            name="add_density",
        )
        mask *= 2
    rp_low, rp_high, response_potential = run(
        potential_body,
        [
            (dens, "v"),
            (swap(dens, mask, "band"), "v"),
            (flat_perturbation, "v"),
            (flat_xc, "v"),
        ],
        [((perts, 1, part_cells), f32)] * 2 + [((perts, planes, gz, gy), f32)],
        limit=3,
        name="potential",
    )

    partial2 = stencil(middle)
    rhs2, gathered2 = margins_in_parts(partial2, halos2, [rp_low, rp_high])
    others2 = [swap(g, 1, "dom") for g in gathered2]
    acc2 = remove_own(gathered2)
    second_res, norms = second_finish(others2, acc2, rhs2, norm1)
    other_norms = swap(norms, 1, "dom")

    def norm_body(one, two, out):
        out[...] = one[...] + two[...]

    (pair_norms,) = run(
        norm_body,
        [(norms, "v"), (other_norms, "v")],
        [((2, columns), f32)],
        limit=1,
        name="norm_pair",
    )
    all_norms = [pair_norms] + [swap(pair_norms, 2 * m, "dom") for m in range(1, chips)]

    def final_body(*refs):
        sums = tree_sum([r[...] for r in refs[:chips]])
        mid, res1, res2, scal, out, steps, blends = refs[chips:]
        ratio = sums[1:2, :] / sums[0:1, :]
        blend = scal[2:3, :] * ratio
        steps[...] = per_row(scal, 2, gy)
        blends[...] = jnp.broadcast_to(blend, (gy, columns)).T
        block = 64 if columns % 64 == 0 else columns

        def rows_step(i, carry):
            rows = pl.ds(pl.multiple_of(i * block, block), block)
            step, mix = steps[rows, :], blends[rows, :]
            for x in range(planes):
                values = []
                for z in range(gz):
                    cut = slice(col(z, x), col(z, x) + gy)
                    values.append(mid[rows, cut] + step * res2[rows, cut] + mix * res1[rows, cut])
                out[rows, x] = jnp.concatenate(values, axis=1).reshape(block, gz, gy)
            return carry

        lax.fori_loop(0, columns // block, rows_step, 0)

    (new_response,) = run(
        final_body,
        [(n, "v") for n in all_norms]
        + [(middle, "v"), (first_res, "v"), (second_res, "v"), (scalars, "v")],
        [((columns, planes, gz, gy), f32)],
        scratch=[pltpu.VMEM((columns, gy), f32), pltpu.VMEM((columns, gy), f32)],
        limit=5,
        name="final",
    )
    return new_response.reshape(response.shape), response_potential


def solution(mesh):
    placed = (
        P(None, "band", "dom", None, None),
        P("band", "dom", None, None),
        P(None, "dom", None, None),
        P("dom", None, None),
        P(None, "dom", None, None),
        P("dom", None, None),
        P("band"),
        P(None, "band"),
        P(None, "band"),
    )
    return jax.shard_map(
        local,
        mesh=mesh,
        in_specs=placed,
        out_specs=(P(None, "band", "dom", None, None), P(None, "dom", None, None)),
        check_vma=False,
    )
```

```python
import jax
import jax.numpy as jnp
from jax import lax
from jax.experimental import pallas as pl
from jax.experimental.pallas import tpu as pltpu
from jax.sharding import PartitionSpec as P

f32 = jnp.float32
bf16 = jnp.bfloat16
near_half = 2.0 / 3.0
far_half = -1.0 / 24.0
centre_half = -3.75
MIB = 1 << 20


def run(body, args, outs, scratch=(), aliases=None, limit=8, name=None):
    kinds = {"v": pltpu.VMEM, "s": pltpu.SMEM, "a": pl.ANY, "h": pltpu.HBM}
    results = pl.pallas_call(
        body,
        in_specs=[pl.BlockSpec(memory_space=kinds[kind]) for _, kind in args],
        out_specs=[pl.BlockSpec(memory_space=kinds[out[2] if len(out) > 2 else "v"]) for out in outs],
        out_shape=[
            pltpu.HBM(out[0], out[1]) if out[2:] == ("h",) else jax.ShapeDtypeStruct(out[0], out[1])
            for out in outs
        ],
        scratch_shapes=list(scratch),
        input_output_aliases=aliases or {},
        compiler_params=pltpu.CompilerParams(vmem_limit_bytes=limit * MIB),
        name=name,
    )(*[array for array, _ in args])
    return list(results)


def tree_sum(terms):
    while len(terms) > 1:
        terms = [terms[i] + terms[i + 1] for i in range(0, len(terms), 2)]
    return terms[0]


def per_row(line, width):
    return jnp.broadcast_to(line, (width, line.shape[1])).T


def dot_nt(a, b):
    return lax.dot_general(a, b, (((1,), (1,)), ((), ())), preferred_element_type=f32)


def dot_nn(a, b):
    return lax.dot_general(a, b, (((1,), (0,)), ((), ())), preferred_element_type=f32)


def local(
    response,
    occupied,
    locked_set,
    potential,
    perturbation,
    xc_kernel,
    energies,
    first_step,
    second_step,
):
    perts, orbs, planes, gz, gy = response.shape
    locked = locked_set.shape[0]
    columns = perts * orbs
    cells = planes * gz * gy
    stripe = planes * gy
    doms = lax.axis_size("dom")
    bands = lax.axis_size("band")
    chips = doms // 2
    half = locked // 2
    piece = half // chips
    part_z = gz // 2
    part_cells = part_z * stripe
    part_edge = part_z * 2 * gy
    position = lax.axis_index("dom")
    where = jnp.stack([position & 1, position >> 1])

    def col(z, x):
        return (z * planes + x) * gy

    def edge(z, k):
        return (z * 2 + k) * gy

    def swap(array, mask, axis):
        count = lax.axis_size(axis)
        return lax.ppermute(array, axis, [(i, i ^ mask) for i in range(count)])

    ahead = [(i, (i + 1) % doms) for i in range(doms)]
    behind = [((i + 1) % doms, i) for i in range(doms)]

    lines = (energies.reshape(1, orbs), first_step, second_step)

    def flatten_body(source, placed, flat, *edges):
        def rows_step(p, carry):
            rows = pl.ds(pl.multiple_of(p * orbs, orbs), orbs)
            for x in range(planes):
                wide = source[rows, x].reshape(orbs, gz * gy)
                for z in range(gz):
                    value = wide[:, z * gy : (z + 1) * gy]
                    flat[rows, col(z, x) : col(z, x) + gy] = value
                    if x < 2:
                        at = edge(z, x)
                        edges[0][rows, at : at + gy] = value.astype(bf16)
                    if x >= planes - 2:
                        at = edge(z, x - planes + 2)
                        edges[1][rows, at : at + gy] = value.astype(bf16)
            return carry

        lax.fori_loop(0, source.shape[0] // orbs, rows_step, 0)

    flat_response, *edges1 = run(
        flatten_body,
        [(response.reshape(columns, planes, gz, gy), "v"), (where, "a")],
        [((columns, cells), f32)]
        + [((columns, gz * 2 * gy), bf16)] * 2,
        limit=8,
        name="flatten",
    )

    def halos_of(low_edge, high_edge):
        return lax.ppermute(high_edge, "dom", ahead), lax.ppermute(low_edge, "dom", behind)

    halos1 = halos_of(*edges1)


    def setup_body(occ, pot, pert, xc, occ_flat, pot_flat, pert_flat, xc_flat):
        for x in range(planes):
            wide = occ[:, x].reshape(orbs, gz * gy)
            for z in range(gz):
                cut = slice(col(z, x), col(z, x) + gy)
                occ_flat[:, cut] = wide[:, z * gy : (z + 1) * gy]
                pot_flat[0:1, cut] = pot[x, z : z + 1, :]
                xc_flat[0:1, cut] = xc[x, z : z + 1, :]
                for p in range(perts):
                    pert_flat[p, 0:1, cut] = pert[p, x, z : z + 1, :]

    flat_occupied, flat_potential, flat_perturbation, flat_xc = run(
        setup_body,
        [(occupied, "v"), (potential, "v"), (perturbation, "v"), (xc_kernel, "v")],
        [
            ((orbs, cells), f32),
            ((1, cells), f32),
            ((perts, 1, cells), f32),
            ((1, cells), f32),
        ],
        limit=2,
        name="setup",
    )

    chunk = min(256, locked)
    chunks = locked // chunk

    def relay_body(source, target, held, ready, in_sems, out_sems):
        def rows_of(i):
            return pl.ds(pl.multiple_of(i * chunk, chunk), chunk)

        def fetch(i):
            slot = lax.rem(i, 3)
            return pltpu.make_async_copy(source.at[rows_of(i)], held.at[slot], in_sems.at[slot])

        def flush(i):
            slot = lax.rem(i, 2)
            return pltpu.make_async_copy(ready.at[slot], target.at[rows_of(i)], out_sems.at[slot])

        fetch(0).start()
        fetch(1).start()

        def step(i, carry):
            @pl.when(i + 2 < chunks)
            def _():
                fetch(i + 2).start()

            @pl.when(i >= 2)
            def _():
                flush(i - 2).wait()

            fetch(i).wait()
            for x in range(planes):
                wide = held[lax.rem(i, 3), :, x].reshape(chunk, gz * gy)
                for z in range(gz):
                    ready[lax.rem(i, 2), :, col(z, x) : col(z, x) + gy] = wide[
                        :, z * gy : (z + 1) * gy
                    ]
            flush(i).start()
            return carry

        lax.fori_loop(0, chunks, step, 0)
        flush(chunks - 2).wait()
        flush(chunks - 1).wait()

    (locked_flat,) = run(
        relay_body,
        [(pltpu.with_memory_space_constraint(locked_set, pltpu.HBM), "h")],
        [((locked, cells), bf16, "h")],
        scratch=[
            pltpu.VMEM((3, chunk, planes, gz, gy), bf16),
            pltpu.VMEM((2, chunk, cells), bf16),
            pltpu.SemaphoreType.DMA((3,)),
            pltpu.SemaphoreType.DMA((2,)),
        ],
        limit=12,
        name="relay",
    )

    locked_flat = pltpu.with_memory_space_constraint(locked_flat, pltpu.HBM)

    def stencil_body(field, pot, scal, out, energy):
        for p in range(perts):
            energy[p * orbs : (p + 1) * orbs, :] = per_row(scal[...], gy)
        block = 32

        def rows_step(i, carry):
            rows = pl.ds(pl.multiple_of(i * block, block), block)
            base = energy[rows, :] + centre_half

            def at(z, x):
                return field[rows, col(z, x) : col(z, x) + gy]

            for z in range(gz):
                for x in range(planes):
                    here = at(z, x)
                    near = pltpu.roll(here, 1, 1) + pltpu.roll(here, gy - 1, 1)
                    far = pltpu.roll(here, 2, 1) + pltpu.roll(here, gy - 2, 1)
                    for d in (-1, 1):
                        if 0 <= x + d < planes:
                            near = near + at(z, x + d)
                        if 0 <= z + d < gz:
                            near = near + at(z + d, x)
                        if 0 <= x + 2 * d < planes:
                            far = far + at(z, x + 2 * d)
                        if 0 <= z + 2 * d < gz:
                            far = far + at(z + 2 * d, x)
                    own = base - pot[0:1, col(z, x) : col(z, x) + gy]
                    out[rows, col(z, x) : col(z, x) + gy] = (
                        own * here + near_half * near + far_half * far
                    )
            return carry

        lax.fori_loop(0, columns // block, rows_step, 0)

    def stencil(field):
        (out,) = run(
            stencil_body,
            [(field, "v"), (flat_potential, "v"), (lines[0], "v")],
            [((columns, cells), f32)],
            scratch=[pltpu.VMEM((columns, gy), f32)],
            limit=1,
            name="stencil",
        )
        return out

    def finish_rhs(first, count, partial, low, high, occ, pot, rhs, rounded):

        def rows_step(p, carry):
            rows = pl.ds(pl.multiple_of(p * orbs, orbs), orbs)
            for inner in range(count):
                for x in range(planes):
                    at = col(first + inner, x)
                    spot = col(inner, x)
                    value = partial[rows, at : at + gy] - pot[p, 0:1, spot : spot + gy] * occ[
                        :, at : at + gy
                    ]

                    def halo(ref, k):
                        start = edge(inner, k)
                        return ref[rows, start : start + gy].astype(f32)

                    if x == 0:
                        value = value + (near_half * halo(low, 1) + far_half * halo(low, 0))
                    if x == 1:
                        value = value + far_half * halo(low, 1)
                    if x == planes - 2:
                        value = value + far_half * halo(high, 0)
                    if x == planes - 1:
                        value = value + (near_half * halo(high, 0) + far_half * halo(high, 1))
                    rhs[rows, at : at + gy] = value
                    rounded[rows, spot : spot + gy] = value.astype(bf16)
            return carry

        lax.fori_loop(0, perts, rows_step, 0)

    def reduce_pieces(own, arrived):
        def pair_body(own_ref, arrived_ref, kept, *sent):
            for m in range(chips):
                cut = slice(m * piece, (m + 1) * piece)
                value = own_ref[:, cut] + arrived_ref[:, cut].astype(f32)
                if m == 0:
                    kept[...] = value
                else:
                    sent[m - 1][...] = value.astype(bf16)

        kept, *sent = run(
            pair_body,
            [(own, "v"), (arrived, "v")],
            [((columns, piece), f32)] + [((columns, piece), bf16)] * (chips - 1),
            limit=6,
            name="margin_pair",
        )
        arrivals = [swap(sent[m - 1], 2 * m, "dom") for m in range(1, chips)]

        def add_body(*refs):
            out = refs[-1]
            out[...] = tree_sum([r[...].astype(f32) for r in refs[:-1]]).astype(bf16)

        (mine,) = run(
            add_body,
            [(kept, "v")] + [(r, "v") for r in arrivals],
            [((columns, piece), bf16)],
            limit=2,
            name="add_pieces",
        )
        gathered = [mine] + [swap(mine, 2 * m, "dom") for m in range(1, chips)]
        return gathered

    def margins_in_parts(partial, halos, pot):
        def column_copies(where_ref, both, first, lock, buf, sems):
            copies = []
            for k in range(len(both)):
                start = (where_ref[0] ^ both[k]) * half
                for m in range(chips):
                    rows = pl.ds(pl.multiple_of(start + (where_ref[1] ^ m) * piece, piece), piece)
                    index = k * chips + m
                    copies.append(
                        pltpu.make_async_copy(
                            lock.at[rows, first * part_cells : (first + 1) * part_cells],
                            buf.at[index],
                            sems.at[index],
                        )
                    )
            return copies

        def scratch_of(count):
            return [
                pltpu.VMEM((count, piece, part_cells), bf16),
                pltpu.SemaphoreType.DMA((count,)),
            ]

        def early_body(where_ref, part_ref, low, high, occ, pot_ref, lock, rhs, out, rounded, buf, sems):
            copies = column_copies(where_ref, (1, 0), 0, lock, buf, sems)
            for copy in copies:
                copy.start()
            finish_rhs(0, part_z, part_ref, low, high, occ, pot_ref, rhs, rounded)
            for m in range(2 * chips):
                copies[m].wait()
                out[:, m * piece : (m + 1) * piece] = dot_nt(rounded[...], buf[m])

        rhs, early = run(
            early_body,
            [
                (where, "s"),
                (partial, "v"),
                (halos[0][0], "v"),
                (halos[0][1], "v"),
                (flat_occupied, "v"),
                (pot[0], "v"),
                (locked_flat, "h"),
            ],
            [((columns, cells), f32), ((columns, locked), f32)],
            scratch=[pltpu.VMEM((columns, part_cells), bf16)] + scratch_of(2 * chips),
            aliases={1: 0},
            limit=24,
            name="margin_early",
        )

        def late_body(
            where_ref, part_ref, low, high, occ, pot_ref, lock, early_ref, rhs, rounded, out, buf, sems
        ):
            copies = column_copies(where_ref, (1,), 1, lock, buf, sems)
            for copy in copies:
                copy.start()
            finish_rhs(part_z, part_z, part_ref, low, high, occ, pot_ref, rhs, rounded)
            for m in range(chips):
                cut = slice(m * piece, (m + 1) * piece)
                copies[m].wait()
                out[:, cut] = (early_ref[:, cut] + dot_nt(rounded[...], buf[m])).astype(bf16)

        rhs, rounded, other = run(
            late_body,
            [
                (where, "s"),
                (rhs, "v"),
                (halos[1][0], "v"),
                (halos[1][1], "v"),
                (flat_occupied, "v"),
                (pot[1], "v"),
                (locked_flat, "h"),
                (early, "v"),
            ],
            [((columns, cells), f32), ((columns, part_cells), bf16), ((columns, half), bf16)],
            scratch=scratch_of(chips),
            aliases={1: 0},
            limit=14,
            name="margin_late",
        )
        arrived = swap(other, 1, "dom")

        def own_body(where_ref, rounded_ref, lock, early_ref, out, buf, sems):
            copies = column_copies(where_ref, (0,), 1, lock, buf, sems)
            for copy in copies:
                copy.start()
            for m in range(chips):
                cut = slice(m * piece, (m + 1) * piece)
                old = early_ref[:, half + m * piece : half + (m + 1) * piece]
                copies[m].wait()
                out[:, cut] = old + dot_nt(rounded_ref[...], buf[m])

        (own,) = run(
            own_body,
            [(where, "s"), (rounded, "v"), (locked_flat, "h"), (early, "v")],
            [((columns, half), f32)],
            scratch=scratch_of(chips),
            limit=14,
            name="margin_late_own",
        )
        return rhs, reduce_pieces(own, arrived)

    def margins(partial, halos, pot):
        low, high = halos

        def piece_copies(where_ref, start, lock, buf, sems):
            copies = []
            for m in range(chips):
                rows = pl.ds(pl.multiple_of(start + (where_ref[1] ^ m) * piece, piece), piece)
                copies.append(pltpu.make_async_copy(lock.at[rows], buf.at[m], sems.at[m]))
            return copies

        piece_scratch = [pltpu.VMEM((chips, piece, cells), bf16), pltpu.SemaphoreType.DMA((chips,))]

        def other_body(
            where_ref, part_ref, low_ref, high_ref, occ, pot_ref, lock, rhs, rounded, out, buf, sems
        ):
            copies = piece_copies(where_ref, (1 - where_ref[0]) * half, lock, buf, sems)
            for copy in copies:
                copy.start()
            finish_rhs(0, gz, part_ref, low_ref, high_ref, occ, pot_ref, rhs, rounded)
            for m in range(chips):
                copies[m].wait()
                out[:, m * piece : (m + 1) * piece] = dot_nt(rounded[...], buf[m]).astype(bf16)

        rhs, rounded, other = run(
            other_body,
            [
                (where, "s"),
                (partial, "v"),
                (low, "v"),
                (high, "v"),
                (flat_occupied, "v"),
                (pot, "v"),
                (locked_flat, "h"),
            ],
            [((columns, cells), f32), ((columns, cells), bf16), ((columns, half), bf16)],
            scratch=piece_scratch,
            aliases={1: 0},
            limit=20,
            name="margin_other",
        )
        arrived = swap(other, 1, "dom")

        def own_body(where_ref, rounded_ref, lock, out, buf, sems):
            copies = piece_copies(where_ref, where_ref[0] * half, lock, buf, sems)
            for copy in copies:
                copy.start()
            for m in range(chips):
                copies[m].wait()
                out[:, m * piece : (m + 1) * piece] = dot_nt(rounded_ref[...], buf[m])

        (own,) = run(
            own_body,
            [(where, "s"), (rounded, "v"), (locked_flat, "h")],
            [((columns, half), f32)],
            scratch=piece_scratch,
            limit=20,
            name="margin_own",
        )

        return rhs, reduce_pieces(own, arrived)

    def collect(where_ref, pieces, held):
        for m, ref in enumerate(pieces):
            at = pl.ds(pl.multiple_of((where_ref[1] ^ m) * piece, piece), piece)
            held[:, at] = ref[...]

    stripe_scratch = [pltpu.VMEM((gz, half, stripe), bf16), pltpu.SemaphoreType.DMA((gz,))]

    def stripe_copy(start, lock, buf, sems, z):
        rows = pl.ds(pl.multiple_of(start, half), half)
        at = pl.ds(pl.multiple_of(z * stripe, stripe), stripe)
        return pltpu.make_async_copy(lock.at[rows, at], buf.at[z], sems.at[z])

    def remove_own(gathered):
        def body(where_ref, *refs):
            pieces, (lock, acc, held, buf, sems) = refs[:chips], refs[chips:]
            start = where_ref[0] * half
            for z in range(gz):
                stripe_copy(start, lock, buf, sems, z).start()
            collect(where_ref, pieces, held)

            def step(z, carry):
                at = pl.ds(pl.multiple_of(z * stripe, stripe), stripe)
                stripe_copy(start, lock, buf, sems, z).wait()
                acc[:, at] = dot_nn(held[...], buf[z])
                return carry

            lax.fori_loop(0, gz, step, 0)

        (acc,) = run(
            body,
            [(where, "s")] + [(g, "v") for g in gathered] + [(locked_flat, "h")],
            [((columns, cells), f32)],
            scratch=[pltpu.VMEM((columns, half), bf16)] + stripe_scratch,
            limit=22,
            name="remove_own",
        )
        return acc

    def line_of(lanes):
        return jnp.sum(lanes.T, axis=0, keepdims=True)

    def squares(value):
        total = value[:, :gy] * value[:, :gy]
        for x in range(1, planes):
            total = total + value[:, x * gy : (x + 1) * gy] * value[:, x * gy : (x + 1) * gy]
        return total

    def first_finish(part, others, acc, rhs, field, before):
        extra = [(array, "v") for array in before]
        base = part * part_z
        origin = 0 if part else base
        width = part_cells * (part + 1)

        def body(where_ref, *refs):
            pieces = refs[:chips]
            lock, acc_ref, rhs_ref, field_ref, occ, scal = refs[chips : chips + 6]
            rest = refs[chips + 6 :]
            old, rest = rest[: len(extra)], rest[len(extra) :]
            res, mid, low, high, dens, norm, held, step_rows, lanes, buf, sems = rest
            start = (1 - where_ref[0]) * half
            for z in range(base, base + part_z):
                stripe_copy(start, lock, buf, sems, z).start()
            collect(where_ref, pieces, held)
            for p in range(perts):
                step_rows[p * orbs : (p + 1) * orbs, :] = per_row(scal[p : p + 1, :], gy)
            lanes[...] = jnp.zeros_like(lanes)

            def step(z, carry):
                at = pl.ds(pl.multiple_of(z * stripe, stripe), stripe)
                stripe_copy(start, lock, buf, sems, z).wait()
                removed = acc_ref[:, at] + dot_nn(held[...], buf[z])
                value = rhs_ref[:, at] - removed
                res[:, at] = value
                lanes[...] += squares(value)
                for x in range(planes):
                    cut = slice(x * gy, (x + 1) * gy)
                    spot = pl.ds(pl.multiple_of(z * stripe + x * gy, gy), gy)
                    new = field_ref[:, spot] + step_rows[...] * value[:, cut]
                    mid[:, spot] = new
                    weight = 2.0 * occ[:, spot]
                    sums = [
                        jnp.sum(weight * new[p * orbs : (p + 1) * orbs], axis=0, keepdims=True)
                        for p in range(perts)
                    ]
                    kept = pl.ds(pl.multiple_of((z - origin) * stripe + x * gy, gy), gy)
                    dens[:, kept] = jnp.concatenate(sums, axis=0).astype(bf16)
                    if x < 2:
                        place = pl.ds(pl.multiple_of(((z - base) * 2 + x) * gy, gy), gy)
                        low[:, place] = new.astype(bf16)
                    if x >= planes - 2:
                        place = pl.ds(pl.multiple_of(((z - base) * 2 + x - planes + 2) * gy, gy), gy)
                        high[:, place] = new.astype(bf16)
                return carry

            lax.fori_loop(base, base + part_z, step, 0)
            norm[...] = line_of(lanes[...])
            if old:
                norm[...] += old[1][...]
                dens[:, :part_cells] = old[0][...]

        return run(
            body,
            [(where, "s")]
            + [(g, "v") for g in others]
            + [
                (locked_flat, "h"),
                (acc, "v"),
                (rhs, "v"),
                (field, "v"),
                (flat_occupied, "v"),
                (lines[1], "v"),
            ]
            + extra,
            [
                ((columns, cells), f32),
                ((columns, cells), f32),
                ((columns, part_edge), bf16),
                ((columns, part_edge), bf16),
                ((perts, width), bf16),
                ((1, columns), f32),
            ],
            scratch=[
                pltpu.VMEM((columns, half), bf16),
                pltpu.VMEM((columns, gy), f32),
                pltpu.VMEM((columns, gy), f32),
            ]
            + stripe_scratch,
            aliases={chips + 3: 0, chips + 4: 1},
            limit=26,
            name="first_finish",
        )

    def second_finish(others, acc, rhs, before):
        def body(where_ref, *refs):
            pieces = refs[:chips]
            lock, acc_ref, rhs_ref, first, res, norm, held, lanes, buf, sems = refs[chips:]
            start = (1 - where_ref[0]) * half
            for z in range(gz):
                stripe_copy(start, lock, buf, sems, z).start()
            collect(where_ref, pieces, held)
            lanes[...] = jnp.zeros_like(lanes)

            def step(z, carry):
                at = pl.ds(pl.multiple_of(z * stripe, stripe), stripe)
                stripe_copy(start, lock, buf, sems, z).wait()
                removed = acc_ref[:, at] + dot_nn(held[...], buf[z])
                value = rhs_ref[:, at] - removed
                res[:, at] = value
                lanes[...] += squares(value)
                return carry

            lax.fori_loop(0, gz, step, 0)
            norm[0:1, :] = first[...]
            norm[1:2, :] = line_of(lanes[...])

        return run(
            body,
            [(where, "s")]
            + [(g, "v") for g in others]
            + [(locked_flat, "h"), (acc, "v"), (rhs, "v"), (before, "v")],
            [((columns, cells), f32), ((2, columns), f32)],
            scratch=[pltpu.VMEM((columns, half), bf16), pltpu.VMEM((columns, gy), f32)]
            + stripe_scratch,
            aliases={chips + 3: 0},
            limit=22,
            name="second_finish",
        )

    partial1 = stencil(flat_response)
    rhs1, gathered1 = margins(partial1, halos1, flat_perturbation)
    others1 = [swap(g, 1, "dom") for g in gathered1]
    acc1 = remove_own(gathered1)
    def add_body(one, two, out):
        out[...] = (one[...].astype(f32) + two[...].astype(f32)).astype(bf16)

    def potential_body(one, two, pert, xc, low, high, native):
        density = one[...].astype(f32) + two[...].astype(f32)
        for z in range(gz):
            for x in range(planes):
                cut = slice(col(z, x), col(z, x) + gy)
                spot = slice(col(z % part_z, x), col(z % part_z, x) + gy)
                flat = low if z < part_z else high
                for p in range(perts):
                    value = pert[p, 0:1, cut] - xc[0:1, cut] * density[p : p + 1, cut]
                    flat[p, 0:1, spot] = value
                    native[p, x, z : z + 1, :] = value

    halos2 = []
    first_res, middle, before = rhs1, flat_response, []
    for part in range(2):
        first_res, middle, low_edge, high_edge, dens, norm1 = first_finish(
            part, others1, acc1, first_res, middle, before
        )
        before = [dens, norm1]
        halos2.append(halos_of(low_edge, high_edge))
    mask = 1
    while 2 * mask < bands:
        (dens,) = run(
            add_body,
            [(dens, "v"), (swap(dens, mask, "band"), "v")],
            [((perts, cells), bf16)],
            limit=2,
            name="add_density",
        )
        mask *= 2
    rp_low, rp_high, response_potential = run(
        potential_body,
        [
            (dens, "v"),
            (swap(dens, mask, "band"), "v"),
            (flat_perturbation, "v"),
            (flat_xc, "v"),
        ],
        [((perts, 1, part_cells), f32)] * 2 + [((perts, planes, gz, gy), f32)],
        limit=3,
        name="potential",
    )

    partial2 = stencil(middle)
    rhs2, gathered2 = margins_in_parts(partial2, halos2, [rp_low, rp_high])
    others2 = [swap(g, 1, "dom") for g in gathered2]
    acc2 = remove_own(gathered2)
    second_res, norms = second_finish(others2, acc2, rhs2, norm1)
    other_norms = swap(norms, 1, "dom")

    def norm_body(one, two, out):
        out[...] = one[...] + two[...]

    (pair_norms,) = run(
        norm_body,
        [(norms, "v"), (other_norms, "v")],
        [((2, columns), f32)],
        limit=1,
        name="norm_pair",
    )
    all_norms = [pair_norms] + [swap(pair_norms, 2 * m, "dom") for m in range(1, chips)]

    def final_body(*refs):
        sums = tree_sum([r[...] for r in refs[:chips]])
        mid, res1, res2, scal, out, steps, blends, ready, sems = refs[chips:]
        ratio = sums[1:2, :] / sums[0:1, :]
        blends[...] = jnp.broadcast_to(ratio, (gy, columns)).T
        for p in range(perts):
            steps[p * orbs : (p + 1) * orbs, :] = per_row(scal[p : p + 1, :], gy)

        def flush(i):
            rows = pl.ds(pl.multiple_of(i * orbs, orbs), orbs)
            return pltpu.make_async_copy(ready.at[i], out.at[rows], sems.at[i])

        def rows_step(i, carry):
            rows = pl.ds(pl.multiple_of(i * orbs, orbs), orbs)
            step, mix = steps[rows, :], blends[rows, :]
            for x in range(planes):
                values = []
                for z in range(gz):
                    cut = slice(col(z, x), col(z, x) + gy)
                    values.append(mid[rows, cut] + step * (res2[rows, cut] + mix * res1[rows, cut]))
                ready[i, :, x] = jnp.concatenate(values, axis=1).reshape(orbs, gz, gy)
            flush(i).start()
            return carry

        lax.fori_loop(0, perts, rows_step, 0)
        for p in range(perts):
            flush(p).wait()

    (new_response,) = run(
        final_body,
        [(n, "v") for n in all_norms]
        + [(middle, "v"), (first_res, "v"), (second_res, "v"), (lines[2], "v")],
        [((columns, planes, gz, gy), f32, "h")],
        scratch=[
            pltpu.VMEM((columns, gy), f32),
            pltpu.VMEM((columns, gy), f32),
            pltpu.VMEM((perts, orbs, planes, gz, gy), f32),
            pltpu.SemaphoreType.DMA((perts,)),
        ],
        limit=8,
        name="final",
    )
    return new_response.reshape(response.shape), response_potential


def solution(mesh):
    placed = (
        P(None, "band", "dom", None, None),
        P("band", "dom", None, None),
        P(None, "dom", None, None),
        P("dom", None, None),
        P(None, "dom", None, None),
        P("dom", None, None),
        P("band"),
        P(None, "band"),
        P(None, "band"),
    )
    return jax.shard_map(
        local,
        mesh=mesh,
        in_specs=placed,
        out_specs=(P(None, "band", "dom", None, None), P(None, "dom", None, None)),
        check_vma=False,
    )
```

```python
import jax
import jax.numpy as jnp
from jax import lax
from jax.experimental import pallas as pl
from jax.experimental.pallas import tpu as pltpu
from jax.sharding import PartitionSpec as P

f32 = jnp.float32
bf16 = jnp.bfloat16
near_half = 2.0 / 3.0
far_half = -1.0 / 24.0
centre_half = -3.75
MIB = 1 << 20


def run(body, args, outs, scratch=(), aliases=None, limit=8, name=None):
    kinds = {"v": pltpu.VMEM, "s": pltpu.SMEM, "a": pl.ANY, "h": pltpu.HBM}
    results = pl.pallas_call(
        body,
        in_specs=[pl.BlockSpec(memory_space=kinds[kind]) for _, kind in args],
        out_specs=[pl.BlockSpec(memory_space=kinds[out[2] if len(out) > 2 else "v"]) for out in outs],
        out_shape=[
            pltpu.HBM(out[0], out[1]) if out[2:] == ("h",) else jax.ShapeDtypeStruct(out[0], out[1])
            for out in outs
        ],
        scratch_shapes=list(scratch),
        input_output_aliases=aliases or {},
        compiler_params=pltpu.CompilerParams(vmem_limit_bytes=limit * MIB),
        name=name,
    )(*[array for array, _ in args])
    return list(results)


def tree_sum(terms):
    while len(terms) > 1:
        terms = [terms[i] + terms[i + 1] for i in range(0, len(terms), 2)]
    return terms[0]


def per_row(line, width):
    return jnp.broadcast_to(line, (width, line.shape[1])).T


def dot_nt(a, b):
    return lax.dot_general(a, b, (((1,), (1,)), ((), ())), preferred_element_type=f32)


def dot_nn(a, b):
    return lax.dot_general(a, b, (((1,), (0,)), ((), ())), preferred_element_type=f32)


def local(
    response,
    occupied,
    locked_set,
    potential,
    perturbation,
    xc_kernel,
    energies,
    first_step,
    second_step,
):
    perts, orbs, planes, gz, gy = response.shape
    locked = locked_set.shape[0]
    columns = perts * orbs
    cells = planes * gz * gy
    stripe = planes * gy
    doms = lax.axis_size("dom")
    bands = lax.axis_size("band")
    chips = doms // 2
    half = locked // 2
    piece = half // chips
    part_z = gz // 2
    part_cells = part_z * stripe
    part_edge = part_z * 2 * gy
    position = lax.axis_index("dom")
    where = jnp.stack([position & 1, position >> 1])

    def col(z, x):
        return (z * planes + x) * gy

    def edge(z, k):
        return (z * 2 + k) * gy

    def swap(array, mask, axis):
        count = lax.axis_size(axis)
        return lax.ppermute(array, axis, [(i, i ^ mask) for i in range(count)])

    ahead = [(i, (i + 1) % doms) for i in range(doms)]
    behind = [((i + 1) % doms, i) for i in range(doms)]

    lines = (energies.reshape(1, orbs), first_step, second_step)

    def flatten_body(source, placed, flat, *edges):
        def rows_step(p, carry):
            rows = pl.ds(pl.multiple_of(p * orbs, orbs), orbs)
            for x in range(planes):
                wide = source[rows, x].reshape(orbs, gz * gy)
                for z in range(gz):
                    value = wide[:, z * gy : (z + 1) * gy]
                    flat[rows, col(z, x) : col(z, x) + gy] = value
                    if x < 2:
                        at = edge(z, x)
                        edges[0][rows, at : at + gy] = value.astype(bf16)
                    if x >= planes - 2:
                        at = edge(z, x - planes + 2)
                        edges[1][rows, at : at + gy] = value.astype(bf16)
            return carry

        lax.fori_loop(0, source.shape[0] // orbs, rows_step, 0)

    flat_response, *edges1 = run(
        flatten_body,
        [(response.reshape(columns, planes, gz, gy), "v"), (where, "a")],
        [((columns, cells), f32)]
        + [((columns, gz * 2 * gy), bf16)] * 2,
        limit=8,
        name="flatten",
    )

    def halos_of(low_edge, high_edge):
        return lax.ppermute(high_edge, "dom", ahead), lax.ppermute(low_edge, "dom", behind)

    halos1 = halos_of(*edges1)


    def setup_body(occ, pot, pert, xc, occ_flat, pot_flat, pert_flat, xc_flat):
        for x in range(planes):
            wide = occ[:, x].reshape(orbs, gz * gy)
            for z in range(gz):
                cut = slice(col(z, x), col(z, x) + gy)
                occ_flat[:, cut] = wide[:, z * gy : (z + 1) * gy]
                pot_flat[0:1, cut] = pot[x, z : z + 1, :]
                xc_flat[0:1, cut] = xc[x, z : z + 1, :]
                for p in range(perts):
                    pert_flat[p, 0:1, cut] = pert[p, x, z : z + 1, :]

    flat_occupied, flat_potential, flat_perturbation, flat_xc = run(
        setup_body,
        [(occupied, "v"), (potential, "v"), (perturbation, "v"), (xc_kernel, "v")],
        [
            ((orbs, cells), f32),
            ((1, cells), f32),
            ((perts, 1, cells), f32),
            ((1, cells), f32),
        ],
        limit=2,
        name="setup",
    )

    chunk = min(256, locked)
    chunks = locked // chunk

    def relay_body(source, target, held, ready, in_sems, out_sems):
        def rows_of(i):
            return pl.ds(pl.multiple_of(i * chunk, chunk), chunk)

        def fetch(i):
            slot = lax.rem(i, 3)
            return pltpu.make_async_copy(source.at[rows_of(i)], held.at[slot], in_sems.at[slot])

        def flush(i):
            slot = lax.rem(i, 2)
            return pltpu.make_async_copy(ready.at[slot], target.at[rows_of(i)], out_sems.at[slot])

        fetch(0).start()
        fetch(1).start()

        def step(i, carry):
            @pl.when(i + 2 < chunks)
            def _():
                fetch(i + 2).start()

            @pl.when(i >= 2)
            def _():
                flush(i - 2).wait()

            fetch(i).wait()
            for x in range(planes):
                wide = held[lax.rem(i, 3), :, x].reshape(chunk, gz * gy)
                for z in range(gz):
                    ready[lax.rem(i, 2), :, col(z, x) : col(z, x) + gy] = wide[
                        :, z * gy : (z + 1) * gy
                    ]
            flush(i).start()
            return carry

        lax.fori_loop(0, chunks, step, 0)
        flush(chunks - 2).wait()
        flush(chunks - 1).wait()

    (locked_flat,) = run(
        relay_body,
        [(pltpu.with_memory_space_constraint(locked_set, pltpu.HBM), "h")],
        [((locked, cells), bf16, "h")],
        scratch=[
            pltpu.VMEM((3, chunk, planes, gz, gy), bf16),
            pltpu.VMEM((2, chunk, cells), bf16),
            pltpu.SemaphoreType.DMA((3,)),
            pltpu.SemaphoreType.DMA((2,)),
        ],
        limit=12,
        name="relay",
    )

    locked_flat = pltpu.with_memory_space_constraint(locked_flat, pltpu.HBM)

    def stencil_body(field, pot, scal, out, energy):
        for p in range(perts):
            energy[p * orbs : (p + 1) * orbs, :] = per_row(scal[...], gy)
        block = 8

        def rows_step(i, carry):
            rows = pl.ds(pl.multiple_of(i * block, block), block)
            base = energy[rows, :] + centre_half

            loaded = {
                (z, x): field[rows, col(z, x) : col(z, x) + gy]
                for z in range(gz)
                for x in range(planes)
            }

            def at(z, x):
                return loaded[z, x]

            for z in range(gz):
                for x in range(planes):
                    here = at(z, x)
                    near = pltpu.roll(here, 1, 1) + pltpu.roll(here, gy - 1, 1)
                    far = pltpu.roll(here, 2, 1) + pltpu.roll(here, gy - 2, 1)
                    for d in (-1, 1):
                        if 0 <= x + d < planes:
                            near = near + at(z, x + d)
                        if 0 <= z + d < gz:
                            near = near + at(z + d, x)
                        if 0 <= x + 2 * d < planes:
                            far = far + at(z, x + 2 * d)
                        if 0 <= z + 2 * d < gz:
                            far = far + at(z + 2 * d, x)
                    own = base - pot[0:1, col(z, x) : col(z, x) + gy]
                    out[rows, col(z, x) : col(z, x) + gy] = (
                        own * here + near_half * near + far_half * far
                    )
            return carry

        lax.fori_loop(0, columns // block, rows_step, 0)

    def stencil(field):
        (out,) = run(
            stencil_body,
            [(field, "v"), (flat_potential, "v"), (lines[0], "v")],
            [((columns, cells), f32)],
            scratch=[pltpu.VMEM((columns, gy), f32)],
            limit=1,
            name="stencil",
        )
        return out

    def finish_rhs(first, count, partial, low, high, occ, pot, rhs, rounded):

        def rows_step(p, carry):
            rows = pl.ds(pl.multiple_of(p * orbs, orbs), orbs)
            for inner in range(count):
                for x in range(planes):
                    at = col(first + inner, x)
                    spot = col(inner, x)
                    value = partial[rows, at : at + gy] - pot[p, 0:1, spot : spot + gy] * occ[
                        :, at : at + gy
                    ]

                    def halo(ref, k):
                        start = edge(inner, k)
                        return ref[rows, start : start + gy].astype(f32)

                    if x == 0:
                        value = value + (near_half * halo(low, 1) + far_half * halo(low, 0))
                    if x == 1:
                        value = value + far_half * halo(low, 1)
                    if x == planes - 2:
                        value = value + far_half * halo(high, 0)
                    if x == planes - 1:
                        value = value + (near_half * halo(high, 0) + far_half * halo(high, 1))
                    rhs[rows, at : at + gy] = value
                    rounded[rows, spot : spot + gy] = value.astype(bf16)
            return carry

        lax.fori_loop(0, perts, rows_step, 0)

    def reduce_pieces(own, arrived):
        def pair_body(own_ref, arrived_ref, kept, *sent):
            for m in range(chips):
                cut = slice(m * piece, (m + 1) * piece)
                value = own_ref[:, cut] + arrived_ref[:, cut].astype(f32)
                if m == 0:
                    kept[...] = value
                else:
                    sent[m - 1][...] = value.astype(bf16)

        kept, *sent = run(
            pair_body,
            [(own, "v"), (arrived, "v")],
            [((columns, piece), f32)] + [((columns, piece), bf16)] * (chips - 1),
            limit=6,
            name="margin_pair",
        )
        arrivals = [swap(sent[m - 1], 2 * m, "dom") for m in range(1, chips)]

        def add_body(*refs):
            out = refs[-1]
            out[...] = tree_sum([r[...].astype(f32) for r in refs[:-1]]).astype(bf16)

        (mine,) = run(
            add_body,
            [(kept, "v")] + [(r, "v") for r in arrivals],
            [((columns, piece), bf16)],
            limit=2,
            name="add_pieces",
        )
        gathered = [mine] + [swap(mine, 2 * m, "dom") for m in range(1, chips)]
        return gathered

    def margins_in_parts(partial, halos, pot):
        def column_copies(where_ref, both, first, lock, buf, sems):
            copies = []
            for k in range(len(both)):
                start = (where_ref[0] ^ both[k]) * half
                for m in range(chips):
                    rows = pl.ds(pl.multiple_of(start + (where_ref[1] ^ m) * piece, piece), piece)
                    index = k * chips + m
                    copies.append(
                        pltpu.make_async_copy(
                            lock.at[rows, first * part_cells : (first + 1) * part_cells],
                            buf.at[index],
                            sems.at[index],
                        )
                    )
            return copies

        def scratch_of(count):
            return [
                pltpu.VMEM((count, piece, part_cells), bf16),
                pltpu.SemaphoreType.DMA((count,)),
            ]

        def early_body(where_ref, part_ref, low, high, occ, pot_ref, lock, rhs, out, rounded, buf, sems):
            copies = column_copies(where_ref, (1, 0), 0, lock, buf, sems)
            for copy in copies:
                copy.start()
            finish_rhs(0, part_z, part_ref, low, high, occ, pot_ref, rhs, rounded)
            for m in range(2 * chips):
                copies[m].wait()
                out[:, m * piece : (m + 1) * piece] = dot_nt(rounded[...], buf[m])

        rhs, early = run(
            early_body,
            [
                (where, "s"),
                (partial, "v"),
                (halos[0][0], "v"),
                (halos[0][1], "v"),
                (flat_occupied, "v"),
                (pot[0], "v"),
                (locked_flat, "h"),
            ],
            [((columns, cells), f32), ((columns, locked), f32)],
            scratch=[pltpu.VMEM((columns, part_cells), bf16)] + scratch_of(2 * chips),
            aliases={1: 0},
            limit=24,
            name="margin_early",
        )

        def late_body(
            where_ref, part_ref, low, high, occ, pot_ref, lock, early_ref, rhs, rounded, out, buf, sems
        ):
            copies = column_copies(where_ref, (1,), 1, lock, buf, sems)
            for copy in copies:
                copy.start()
            finish_rhs(part_z, part_z, part_ref, low, high, occ, pot_ref, rhs, rounded)
            for m in range(chips):
                cut = slice(m * piece, (m + 1) * piece)
                copies[m].wait()
                out[:, cut] = (early_ref[:, cut] + dot_nt(rounded[...], buf[m])).astype(bf16)

        rhs, rounded, other = run(
            late_body,
            [
                (where, "s"),
                (rhs, "v"),
                (halos[1][0], "v"),
                (halos[1][1], "v"),
                (flat_occupied, "v"),
                (pot[1], "v"),
                (locked_flat, "h"),
                (early, "v"),
            ],
            [((columns, cells), f32), ((columns, part_cells), bf16), ((columns, half), bf16)],
            scratch=scratch_of(chips),
            aliases={1: 0},
            limit=14,
            name="margin_late",
        )
        arrived = swap(other, 1, "dom")

        def own_body(where_ref, rounded_ref, lock, early_ref, out, buf, sems):
            copies = column_copies(where_ref, (0,), 1, lock, buf, sems)
            for copy in copies:
                copy.start()
            for m in range(chips):
                cut = slice(m * piece, (m + 1) * piece)
                old = early_ref[:, half + m * piece : half + (m + 1) * piece]
                copies[m].wait()
                out[:, cut] = old + dot_nt(rounded_ref[...], buf[m])

        (own,) = run(
            own_body,
            [(where, "s"), (rounded, "v"), (locked_flat, "h"), (early, "v")],
            [((columns, half), f32)],
            scratch=scratch_of(chips),
            limit=14,
            name="margin_late_own",
        )
        return rhs, reduce_pieces(own, arrived)

    def margins(partial, halos, pot):
        low, high = halos

        def piece_copies(where_ref, start, lock, buf, sems):
            copies = []
            for m in range(chips):
                rows = pl.ds(pl.multiple_of(start + (where_ref[1] ^ m) * piece, piece), piece)
                copies.append(pltpu.make_async_copy(lock.at[rows], buf.at[m], sems.at[m]))
            return copies

        piece_scratch = [pltpu.VMEM((chips, piece, cells), bf16), pltpu.SemaphoreType.DMA((chips,))]

        def other_body(
            where_ref, part_ref, low_ref, high_ref, occ, pot_ref, lock, rhs, rounded, out, buf, sems
        ):
            copies = piece_copies(where_ref, (1 - where_ref[0]) * half, lock, buf, sems)
            for copy in copies:
                copy.start()
            finish_rhs(0, gz, part_ref, low_ref, high_ref, occ, pot_ref, rhs, rounded)
            for m in range(chips):
                copies[m].wait()
                out[:, m * piece : (m + 1) * piece] = dot_nt(rounded[...], buf[m]).astype(bf16)

        rhs, rounded, other = run(
            other_body,
            [
                (where, "s"),
                (partial, "v"),
                (low, "v"),
                (high, "v"),
                (flat_occupied, "v"),
                (pot, "v"),
                (locked_flat, "h"),
            ],
            [((columns, cells), f32), ((columns, cells), bf16), ((columns, half), bf16)],
            scratch=piece_scratch,
            aliases={1: 0},
            limit=20,
            name="margin_other",
        )
        arrived = swap(other, 1, "dom")

        def own_body(where_ref, rounded_ref, lock, out, buf, sems):
            copies = piece_copies(where_ref, where_ref[0] * half, lock, buf, sems)
            for copy in copies:
                copy.start()
            for m in range(chips):
                copies[m].wait()
                out[:, m * piece : (m + 1) * piece] = dot_nt(rounded_ref[...], buf[m])

        (own,) = run(
            own_body,
            [(where, "s"), (rounded, "v"), (locked_flat, "h")],
            [((columns, half), f32)],
            scratch=piece_scratch,
            limit=20,
            name="margin_own",
        )

        return rhs, reduce_pieces(own, arrived)

    def collect(where_ref, pieces, held):
        for m, ref in enumerate(pieces):
            at = pl.ds(pl.multiple_of((where_ref[1] ^ m) * piece, piece), piece)
            held[:, at] = ref[...]

    stripe_scratch = [pltpu.VMEM((gz, half, stripe), bf16), pltpu.SemaphoreType.DMA((gz,))]

    def stripe_copy(start, lock, buf, sems, z):
        rows = pl.ds(pl.multiple_of(start, half), half)
        at = pl.ds(pl.multiple_of(z * stripe, stripe), stripe)
        return pltpu.make_async_copy(lock.at[rows, at], buf.at[z], sems.at[z])

    def remove_own(gathered):
        def body(where_ref, *refs):
            pieces, (lock, acc, held, buf, sems) = refs[:chips], refs[chips:]
            start = where_ref[0] * half
            for z in range(gz):
                stripe_copy(start, lock, buf, sems, z).start()
            collect(where_ref, pieces, held)

            def step(z, carry):
                at = pl.ds(pl.multiple_of(z * stripe, stripe), stripe)
                stripe_copy(start, lock, buf, sems, z).wait()
                acc[:, at] = dot_nn(held[...], buf[z])
                return carry

            lax.fori_loop(0, gz, step, 0)

        (acc,) = run(
            body,
            [(where, "s")] + [(g, "v") for g in gathered] + [(locked_flat, "h")],
            [((columns, cells), f32)],
            scratch=[pltpu.VMEM((columns, half), bf16)] + stripe_scratch,
            limit=22,
            name="remove_own",
        )
        return acc

    def line_of(lanes):
        return jnp.sum(lanes.T, axis=0, keepdims=True)

    def squares(value):
        total = value[:, :gy] * value[:, :gy]
        for x in range(1, planes):
            total = total + value[:, x * gy : (x + 1) * gy] * value[:, x * gy : (x + 1) * gy]
        return total

    def first_finish(part, others, acc, rhs, field, before):
        extra = [(array, "v") for array in before]
        base = part * part_z
        origin = 0 if part else base
        width = part_cells * (part + 1)

        def body(where_ref, *refs):
            pieces = refs[:chips]
            lock, acc_ref, rhs_ref, field_ref, occ, scal = refs[chips : chips + 6]
            rest = refs[chips + 6 :]
            old, rest = rest[: len(extra)], rest[len(extra) :]
            res, mid, low, high, dens, norm, held, step_rows, lanes, buf, sems = rest
            start = (1 - where_ref[0]) * half
            for z in range(base, base + part_z):
                stripe_copy(start, lock, buf, sems, z).start()
            collect(where_ref, pieces, held)
            for p in range(perts):
                step_rows[p * orbs : (p + 1) * orbs, :] = per_row(scal[p : p + 1, :], gy)
            lanes[...] = jnp.zeros_like(lanes)

            def step(z, carry):
                at = pl.ds(pl.multiple_of(z * stripe, stripe), stripe)
                stripe_copy(start, lock, buf, sems, z).wait()
                removed = acc_ref[:, at] + dot_nn(held[...], buf[z])
                value = rhs_ref[:, at] - removed
                res[:, at] = value
                lanes[...] += squares(value)
                for x in range(planes):
                    cut = slice(x * gy, (x + 1) * gy)
                    spot = pl.ds(pl.multiple_of(z * stripe + x * gy, gy), gy)
                    new = field_ref[:, spot] + step_rows[...] * value[:, cut]
                    mid[:, spot] = new
                    weight = 2.0 * occ[:, spot]
                    sums = [
                        jnp.sum(weight * new[p * orbs : (p + 1) * orbs], axis=0, keepdims=True)
                        for p in range(perts)
                    ]
                    kept = pl.ds(pl.multiple_of((z - origin) * stripe + x * gy, gy), gy)
                    dens[:, kept] = jnp.concatenate(sums, axis=0).astype(bf16)
                    if x < 2:
                        place = pl.ds(pl.multiple_of(((z - base) * 2 + x) * gy, gy), gy)
                        low[:, place] = new.astype(bf16)
                    if x >= planes - 2:
                        place = pl.ds(pl.multiple_of(((z - base) * 2 + x - planes + 2) * gy, gy), gy)
                        high[:, place] = new.astype(bf16)
                return carry

            lax.fori_loop(base, base + part_z, step, 0)
            norm[...] = line_of(lanes[...])
            if old:
                norm[...] += old[1][...]
                dens[:, :part_cells] = old[0][...]

        return run(
            body,
            [(where, "s")]
            + [(g, "v") for g in others]
            + [
                (locked_flat, "h"),
                (acc, "v"),
                (rhs, "v"),
                (field, "v"),
                (flat_occupied, "v"),
                (lines[1], "v"),
            ]
            + extra,
            [
                ((columns, cells), f32),
                ((columns, cells), f32),
                ((columns, part_edge), bf16),
                ((columns, part_edge), bf16),
                ((perts, width), bf16),
                ((1, columns), f32),
            ],
            scratch=[
                pltpu.VMEM((columns, half), bf16),
                pltpu.VMEM((columns, gy), f32),
                pltpu.VMEM((columns, gy), f32),
            ]
            + stripe_scratch,
            aliases={chips + 3: 0, chips + 4: 1},
            limit=26,
            name="first_finish",
        )

    def second_finish(others, acc, rhs, before):
        def body(where_ref, *refs):
            pieces = refs[:chips]
            lock, acc_ref, rhs_ref, first, res, norm, held, lanes, buf, sems = refs[chips:]
            start = (1 - where_ref[0]) * half
            for z in range(gz):
                stripe_copy(start, lock, buf, sems, z).start()
            collect(where_ref, pieces, held)
            lanes[...] = jnp.zeros_like(lanes)

            def step(z, carry):
                at = pl.ds(pl.multiple_of(z * stripe, stripe), stripe)
                stripe_copy(start, lock, buf, sems, z).wait()
                removed = acc_ref[:, at] + dot_nn(held[...], buf[z])
                value = rhs_ref[:, at] - removed
                res[:, at] = value
                lanes[...] += squares(value)
                return carry

            lax.fori_loop(0, gz, step, 0)
            norm[0:1, :] = first[...]
            norm[1:2, :] = line_of(lanes[...])

        return run(
            body,
            [(where, "s")]
            + [(g, "v") for g in others]
            + [(locked_flat, "h"), (acc, "v"), (rhs, "v"), (before, "v")],
            [((columns, cells), f32), ((2, columns), f32)],
            scratch=[pltpu.VMEM((columns, half), bf16), pltpu.VMEM((columns, gy), f32)]
            + stripe_scratch,
            aliases={chips + 3: 0},
            limit=22,
            name="second_finish",
        )

    partial1 = stencil(flat_response)
    rhs1, gathered1 = margins(partial1, halos1, flat_perturbation)
    others1 = [swap(g, 1, "dom") for g in gathered1]
    acc1 = remove_own(gathered1)
    def add_body(one, two, out):
        out[...] = (one[...].astype(f32) + two[...].astype(f32)).astype(bf16)

    def potential_body(one, two, pert, xc, low, high, native):
        density = one[...].astype(f32) + two[...].astype(f32)
        for z in range(gz):
            for x in range(planes):
                cut = slice(col(z, x), col(z, x) + gy)
                spot = slice(col(z % part_z, x), col(z % part_z, x) + gy)
                flat = low if z < part_z else high
                for p in range(perts):
                    value = pert[p, 0:1, cut] - xc[0:1, cut] * density[p : p + 1, cut]
                    flat[p, 0:1, spot] = value
                    native[p, x, z : z + 1, :] = value

    halos2 = []
    first_res, middle, before = rhs1, flat_response, []
    for part in range(2):
        first_res, middle, low_edge, high_edge, dens, norm1 = first_finish(
            part, others1, acc1, first_res, middle, before
        )
        before = [dens, norm1]
        halos2.append(halos_of(low_edge, high_edge))
    mask = 1
    while 2 * mask < bands:
        (dens,) = run(
            add_body,
            [(dens, "v"), (swap(dens, mask, "band"), "v")],
            [((perts, cells), bf16)],
            limit=2,
            name="add_density",
        )
        mask *= 2
    rp_low, rp_high, response_potential = run(
        potential_body,
        [
            (dens, "v"),
            (swap(dens, mask, "band"), "v"),
            (flat_perturbation, "v"),
            (flat_xc, "v"),
        ],
        [((perts, 1, part_cells), f32)] * 2 + [((perts, planes, gz, gy), f32)],
        limit=3,
        name="potential",
    )

    partial2 = stencil(middle)
    rhs2, gathered2 = margins_in_parts(partial2, halos2, [rp_low, rp_high])
    others2 = [swap(g, 1, "dom") for g in gathered2]
    acc2 = remove_own(gathered2)
    second_res, norms = second_finish(others2, acc2, rhs2, norm1)
    other_norms = swap(norms, 1, "dom")

    def norm_body(one, two, out):
        out[...] = one[...] + two[...]

    (pair_norms,) = run(
        norm_body,
        [(norms, "v"), (other_norms, "v")],
        [((2, columns), f32)],
        limit=1,
        name="norm_pair",
    )
    all_norms = [pair_norms] + [swap(pair_norms, 2 * m, "dom") for m in range(1, chips)]

    def final_body(*refs):
        sums = tree_sum([r[...] for r in refs[:chips]])
        mid, res1, res2, scal, out, steps, blends, ready, sems = refs[chips:]
        ratio = sums[1:2, :] / sums[0:1, :]
        blends[...] = jnp.broadcast_to(ratio, (gy, columns)).T
        for p in range(perts):
            steps[p * orbs : (p + 1) * orbs, :] = per_row(scal[p : p + 1, :], gy)

        def flush(i):
            rows = pl.ds(pl.multiple_of(i * orbs, orbs), orbs)
            return pltpu.make_async_copy(ready.at[i], out.at[rows], sems.at[i])

        def rows_step(i, carry):
            rows = pl.ds(pl.multiple_of(i * orbs, orbs), orbs)
            step, mix = steps[rows, :], blends[rows, :]
            for x in range(planes):
                values = []
                for z in range(gz):
                    cut = slice(col(z, x), col(z, x) + gy)
                    values.append(mid[rows, cut] + step * (res2[rows, cut] + mix * res1[rows, cut]))
                ready[i, :, x] = jnp.concatenate(values, axis=1).reshape(orbs, gz, gy)
            flush(i).start()
            return carry

        lax.fori_loop(0, perts, rows_step, 0)
        for p in range(perts):
            flush(p).wait()

    (new_response,) = run(
        final_body,
        [(n, "v") for n in all_norms]
        + [(middle, "v"), (first_res, "v"), (second_res, "v"), (lines[2], "v")],
        [((columns, planes, gz, gy), f32, "h")],
        scratch=[
            pltpu.VMEM((columns, gy), f32),
            pltpu.VMEM((columns, gy), f32),
            pltpu.VMEM((perts, orbs, planes, gz, gy), f32),
            pltpu.SemaphoreType.DMA((perts,)),
        ],
        limit=8,
        name="final",
    )
    return new_response.reshape(response.shape), response_potential


def solution(mesh):
    placed = (
        P(None, "band", "dom", None, None),
        P("band", "dom", None, None),
        P(None, "dom", None, None),
        P("dom", None, None),
        P(None, "dom", None, None),
        P("dom", None, None),
        P("band"),
        P(None, "band"),
        P(None, "band"),
    )
    return jax.shard_map(
        local,
        mesh=mesh,
        in_specs=placed,
        out_specs=(P(None, "band", "dom", None, None), P(None, "dom", None, None)),
        check_vma=False,
    )
```
